256 devices in a mesh: ctx: 32 (over x, z), tp: 8 (over y, core).
Axes of the slice: x: 4, y: 4, z: 8, core: 2. Of those that a mesh axis runs over, the one named last changes fastest.
Arguments:
- projected: bfloat16 [4096, 3, 4096], P('ctx', None, 'tp'), may hold values from -6 to 6
- short_filter: float32 [7, 3, 4096], P(None, None, 'tp'), may hold values from -2.4 to 2.4
- long_filter: bfloat16 [256, 2048], P('tp'), may hold values from -0.26516504 to 0.26516504
- out_weight: bfloat16 [4096, 8192], P('tp'), may hold values from -0.09375 to 0.09375
Outputs:
- layer_out: bfloat16 [4096, 8192], P('ctx', 'tp')
The draws below stay inside these ranges and needn't reach their ends.
All inputs are finite; a program needn't handle non-finite values.
Results may differ from the reference program's by a relative error of at most 0.015.
Values may be sent and summed in bfloat16 or wider, within the bound.
No kernel may reach another device: no remote copies, remote signals or barrier semaphores. Data moves between devices by JAX's collectives and lax.ppermute only.
A program may use at most 64 MiB of HBM per device.

```python
import math
import jax
import jax.numpy as jnp
from jax import lax

C = 4096
DOUT = 8192
GSIZE = 16
TAPS = 7
TOKENS = 4096
FILT = 2048
GROUPS = 256
N_TP = 8


def draw_long_filter(key, part):
    key_rate = jax.random.fold_in(key, 11)
    key_noise = jax.random.fold_in(key, 12)
    rates = jnp.exp(jax.random.uniform(key_rate, (GROUPS, 1), jnp.float32, math.log(0.2), math.log(4.0)))
    position = jnp.arange(FILT, dtype=jnp.float32)[None, :] / FILT
    envelope = jnp.exp(-rates * position) * jnp.sqrt(2.0 * rates / FILT / (1.0 - jnp.exp(-2.0 * rates)))
    noise = jnp.clip(jax.random.normal(key_noise, (GROUPS, FILT), jnp.float32), -4.0, 4.0)
    return (noise * envelope).astype(jnp.bfloat16)


def block_scale(key, dims, pieces, low, high):
    gain, own = 1.0, jax.random.fold_in(key, 6)
    for dim, parts in pieces:
        heights = jnp.exp(jax.random.uniform(jax.random.fold_in(own, dim), (parts,), jnp.float32, low / len(pieces), high / len(pieces)))
        gain = gain * jnp.repeat(heights, dims[dim] // parts).reshape([-1 if axis == dim else 1 for axis in range(len(dims))])
    return gain


def bell_draw(own_key, dims, spread, limit, shards=(), held_as=jnp.bfloat16):
    array = spread * jax.random.normal(own_key, dims, jnp.float32)
    if shards:
        array = array * block_scale(own_key, dims, shards, -0.22, 0.18)
    return jnp.clip(array, -limit, limit).astype(held_as)


def setup_inputs(seed: int = 0) -> dict:
    streams_of = jax.random.split(jax.random.key(seed), 5)
    return {
        "projected": bell_draw(streams_of[0], (TOKENS, 3, C), 1.0, 6.0, ((0, 32), (2, 8))),
        "short_filter": bell_draw(streams_of[1], (TAPS, 3, C), 0.4, 2.4, ((2, 8),), jnp.float32),
        "long_filter": draw_long_filter(jax.random.fold_in(streams_of[4], 71), 0),
        "out_weight": bell_draw(streams_of[3], (C, DOUT), C ** -0.5, 0.09375, ((0, 8),)),
    }


def reference(projected, short_filter, long_filter, out_weight):
    features = projected.astype(jnp.float32)
    padded = jnp.pad(features, ((TAPS - 1, 0), (0, 0), (0, 0)))
    conved = short_filter[0] * padded[TAPS - 1:TAPS - 1 + TOKENS]
    for offset in range(1, TAPS):
        conved = conved + short_filter[offset] * padded[TAPS - 1 - offset:TAPS - 1 - offset + TOKENS]
    values = (conved[:, 1, :] * conved[:, 2, :]).astype(jnp.bfloat16)
    channel_taps = jnp.repeat(long_filter.astype(jnp.float32), GSIZE, axis=0).T
    length = 2 * TOKENS
    spectrum = jnp.fft.rfft(values.astype(jnp.float32), n=length, axis=0) * jnp.fft.rfft(channel_taps, n=length, axis=0)
    mixed = jnp.fft.irfft(spectrum, n=length, axis=0)[:TOKENS]
    hidden = (conved[:, 0, :] * mixed).astype(jnp.bfloat16)
    share = C // N_TP
    total = jnp.zeros((TOKENS, DOUT), jnp.float32)
    for group in range(N_TP):
        partial_sum = jnp.dot(hidden[:, group * share:(group + 1) * share], out_weight[group * share:(group + 1) * share], preferred_element_type=jnp.float32)
        rounded = lax.optimization_barrier(partial_sum.astype(jnp.bfloat16))
        total = total + rounded.astype(jnp.float32)
    return total.astype(jnp.bfloat16)
```

```python
import functools

import jax
import jax.numpy as jnp
from jax import lax
from jax.experimental import pallas as pl
from jax.experimental.pallas import tpu as pltpu
from jax.sharding import PartitionSpec as P

BF = jnp.bfloat16
F32 = jnp.float32


def pack_kernel(x_ref, out_ref, *, gsize):
    feats, tokens, channels = x_ref.shape
    for f in range(feats):
        for j in range(0, channels, 128):
            block = x_ref[f, :, j : j + 128].T
            out_ref[j // gsize : (j + 128) // gsize, f * gsize : (f + 1) * gsize, :] = block.reshape(
                128 // gsize, gsize, tokens
            )


def conv_kernel(meta_ref, x_ref, sf_ref, lf_ref, out_ref, z_ref, g_ref, gate_ref, *, gsize, chunk):
    blocks, _, tok = x_ref.shape
    taps = sf_ref.shape[1]
    reach = lf_ref.shape[2]
    lags = reach // tok + 1
    offset = meta_ref[1] * gsize
    row = lax.broadcasted_iota(jnp.int32, (gsize, 128), 0)
    lane16 = lax.broadcasted_iota(jnp.int32, (gsize, 128), 1)
    pick = lane16 == row + offset
    coef = [
        [
            jnp.broadcast_to(
                jnp.sum(jnp.where(pick, sf_ref[p, d : d + 1, :], 0.0), axis=1, keepdims=True), (gsize, tok)
            )[None]
            for d in range(taps)
        ]
        for p in range(3)
    ]
    s_i = lax.broadcasted_iota(jnp.int32, (tok, tok), 0)
    t_i = lax.broadcasted_iota(jnp.int32, (tok, tok), 1)
    upper = t_i >= s_i
    before = jnp.zeros((tok, tok), F32)
    for k in range(lags):
        if k < lags - 1:
            taps_k = lf_ref[0, :, k * tok : (k + 1) * tok].astype(F32)
            here = pltpu.roll(jnp.broadcast_to(taps_k, (tok, tok)), 0, 1, stride=1, stride_axis=0)
        else:
            here = jnp.zeros((tok, tok), F32)
        g_ref[k * tok : (k + 1) * tok, :] = jnp.where(upper, here, before).astype(BF)
        before = here
    for k in range(1, lags):
        z_ref[0 : k * gsize, k * tok : (k + 1) * tok] = jnp.zeros((k * gsize, tok), BF)
    lane = lax.broadcasted_iota(jnp.int32, (chunk, gsize, tok), 2)
    for a in range(0, blocks, chunk):
        conved = []
        for p in range(3):
            rows = slice(p * gsize, (p + 1) * gsize)
            if a == 0:
                now = x_ref[0:chunk, rows, :].astype(F32)
                slab = jnp.concatenate([jnp.zeros((1, gsize, tok), F32), now], axis=0)
            else:
                slab = x_ref[a - 1 : a + chunk, rows, :].astype(F32)
            total = coef[p][0] * slab[1:]
            flat = slab.reshape((chunk + 1) * gsize, tok)
            for d in range(1, taps):
                turned = pltpu.roll(flat, d, 1).reshape(chunk + 1, gsize, tok)
                total = total + coef[p][d] * jnp.where(lane < d, turned[:chunk], turned[1:])
            conved.append(total)
        gate_ref[a * gsize : (a + chunk) * gsize, :] = conved[0].reshape(chunk * gsize, tok)
        values = (conved[1] * conved[2]).reshape(chunk * gsize, tok).astype(BF)
        for k in range(lags):
            first = (a + k) * gsize
            count = min(chunk * gsize, blocks * gsize - first)
            if count > 0:
                z_ref[first : first + count, k * tok : (k + 1) * tok] = values[:count]
    mixed = jnp.dot(z_ref[...], g_ref[...], preferred_element_type=F32)
    out_ref[...] = (gate_ref[...] * mixed).astype(BF).reshape(blocks, gsize, tok)


def project_kernel(meta_ref, h_ref, w_ref, out_ref, ht_ref):
    @pl.when(pl.program_id(0) == 0)
    def _():
        ht_ref[...] = h_ref[...].T

    out_ref[0] = jnp.dot(ht_ref[...], w_ref[...], preferred_element_type=F32).astype(BF)


def body(projected, short_filter, long_filter, out_weight):
    tok, feats, channels = projected.shape
    groups, reach = long_filter.shape
    gsize = channels // groups
    taps = short_filter.shape[0]
    dout = out_weight.shape[1]
    n_tp = lax.axis_size("tp")
    cols = dout // n_tp
    blocks = lax.axis_size("ctx")
    me = lax.axis_index("ctx")
    tp = lax.axis_index("tp")
    y, core = tp // 2, tp % 2
    order = [y, y ^ 1, 3 - y, 3 - (y ^ 1)]
    meta = jnp.stack([me, me % 8] + [2 * q + core for q in order] + [2 * q + 1 - core for q in order]).astype(
        jnp.int32
    )

    packed = pl.pallas_call(
        functools.partial(pack_kernel, gsize=gsize),
        out_shape=jax.ShapeDtypeStruct((groups, feats * gsize, tok), BF),
        name="pack",
    )(projected.transpose(1, 0, 2))
    spread = lax.all_to_all(packed, "ctx", 0, 0, tiled=True)
    lags = reach // tok + 1
    hidden = pl.pallas_call(
        functools.partial(conv_kernel, gsize=gsize, chunk=4),
        grid_spec=pltpu.PrefetchScalarGridSpec(
            num_scalar_prefetch=1,
            grid=(1,),
            in_specs=[
                pl.BlockSpec((blocks, feats * gsize, tok), lambda i, m: (0, 0, 0)),
                pl.BlockSpec((feats, taps, 128), lambda i, m: (0, 0, m[0] // 8)),
                pl.BlockSpec((1, 1, reach), lambda i, m: (m[0], 0, 0)),
            ],
            out_specs=pl.BlockSpec((blocks, gsize, tok), lambda i, m: (0, 0, 0)),
            scratch_shapes=[
                pltpu.VMEM((blocks * gsize, lags * tok), BF),
                pltpu.VMEM((lags * tok, tok), BF),
                pltpu.VMEM((blocks * gsize, tok), F32),
            ],
        ),
        out_shape=jax.ShapeDtypeStruct((blocks, gsize, tok), BF),
        name="conv",
    )(meta, spread, short_filter.transpose(1, 0, 2), long_filter.reshape(groups, 1, reach))
    hidden = lax.all_to_all(hidden, "ctx", 0, 0, tiled=True).reshape(channels, tok)

    def project(first):
        return pl.pallas_call(
            project_kernel,
            grid_spec=pltpu.PrefetchScalarGridSpec(
                num_scalar_prefetch=1,
                grid=(4,),
                in_specs=[
                    pl.BlockSpec((channels, tok), lambda i, m: (0, 0)),
                    pl.BlockSpec((channels, cols), lambda i, m: (0, m[first + i])),
                ],
                out_specs=pl.BlockSpec((1, tok, cols), lambda i, m: (i, 0, 0)),
                scratch_shapes=[pltpu.VMEM((tok, channels), BF)],
            ),
            out_shape=jax.ShapeDtypeStruct((4, tok, cols), BF),
            name="project",
        )(meta, hidden, out_weight)

    other = project(6)
    mine = project(2)

    def swap(x, peer):
        return lax.ppermute(x, "tp", [(i, peer(i)) for i in range(n_tp)])

    def near(i):
        return i ^ 2

    def far(i):
        return (3 - i // 2) * 2 + i % 2

    half = tok // 2
    got = swap(other, lambda i: i ^ 1)

    def joined(q, lo):
        return got[q, lo : lo + half].astype(F32) + mine[q, lo : lo + half].astype(F32)

    a_in = swap(jnp.stack([joined(1, 0), joined(3, 0)]).astype(BF), near)
    b_in = swap(jnp.stack([joined(2, half), joined(3, half)]).astype(BF), far)
    a_out = swap((a_in[1].astype(F32) + joined(2, 0)).astype(BF), far)
    b_out = swap((b_in[1].astype(F32) + joined(1, half)).astype(BF), near)
    top = a_in[0].astype(F32) + joined(0, 0) + a_out.astype(F32)
    bottom = b_in[0].astype(F32) + joined(0, half) + b_out.astype(F32)
    return jnp.concatenate([top, bottom], axis=0).astype(BF)


def solution(mesh):
    return jax.shard_map(
        body,
        mesh=mesh,
        in_specs=(P("ctx", None, "tp"), P(None, None, "tp"), P("tp", None), P("tp", None)),
        out_specs=P("ctx", "tp"),
        check_vma=False,
    )
```

```python
import functools

import jax
import jax.numpy as jnp
from jax import lax
from jax.experimental import pallas as pl
from jax.experimental.pallas import tpu as pltpu
from jax.sharding import PartitionSpec as P

BF = jnp.bfloat16
F32 = jnp.float32
VMEM = pl.BlockSpec(memory_space=pltpu.VMEM)
HBM = pl.BlockSpec(memory_space=pltpu.HBM)


def in_hbm(x):
    return pltpu.with_memory_space_constraint(x, pltpu.HBM)


def shaped(shape, dtype=BF):
    return jax.ShapeDtypeStruct(shape, dtype)


def call(kernel, out_shape, in_specs, scratch=(), limit=16, flops=0, nbytes=0):
    many = isinstance(out_shape, (list, tuple))
    return pl.pallas_call(
        kernel,
        out_shape=out_shape,
        in_specs=in_specs,
        out_specs=[VMEM] * len(out_shape) if many else VMEM,
        scratch_shapes=list(scratch),
        compiler_params=pltpu.CompilerParams(vmem_limit_bytes=limit << 20),
        cost_estimate=pl.CostEstimate(flops=flops, bytes_accessed=nbytes, transcendentals=0),
    )


def pack_kernel(x_hbm, sf_hbm, lf_hbm, out_ref, sf_ref, lf_ref, x_ref, sems, *, gsize):
    feats, tokens, channels = x_hbm.shape
    copies = [pltpu.make_async_copy(x_hbm.at[f], x_ref.at[f], sems.at[f]) for f in range(feats)]
    copies.append(pltpu.make_async_copy(sf_hbm, sf_ref, sems.at[feats]))
    copies.append(pltpu.make_async_copy(lf_hbm, lf_ref, sems.at[feats + 1]))
    for copy in copies:
        copy.start()
    for f in range(feats):
        copies[f].wait()
        for j in range(0, channels, 128):
            block = x_ref[f, :, j : j + 128].T
            out_ref[j // gsize : (j + 128) // gsize, f * gsize : (f + 1) * gsize, :] = block.reshape(
                128 // gsize, gsize, tokens
            )
    copies[feats].wait()
    copies[feats + 1].wait()


def conv_kernel(x_ref, sf_ref, lf_ref, w_hbm, out_ref, w_ref, z_ref, g_ref, gate_ref, w_sem, *, gsize, chunk):
    w_copy = pltpu.make_async_copy(w_hbm, w_ref, w_sem)
    w_copy.start()
    blocks, _, tok = x_ref.shape
    _, taps, channels = sf_ref.shape
    groups, reach = lf_ref.shape
    lags = reach // tok + 1
    me = lax.axis_index("ctx")
    row = lax.broadcasted_iota(jnp.int32, (gsize, channels), 0)
    col = lax.broadcasted_iota(jnp.int32, (gsize, channels), 1)
    pick = col == row + me * gsize
    coef = [
        [
            jnp.broadcast_to(
                jnp.sum(jnp.where(pick, sf_ref[p, d : d + 1, :], 0.0), axis=1, keepdims=True), (gsize, tok)
            )[None]
            for d in range(taps)
        ]
        for p in range(3)
    ]
    s_i = lax.broadcasted_iota(jnp.int32, (tok, tok), 0)
    t_i = lax.broadcasted_iota(jnp.int32, (tok, tok), 1)
    upper = t_i >= s_i
    mine = lax.broadcasted_iota(jnp.int32, (groups, tok), 0) == me
    before = jnp.zeros((tok, tok), F32)
    for k in range(lags):
        if k < lags - 1:
            taps_k = lf_ref[:, k * tok : (k + 1) * tok].astype(F32)
            taps_k = jnp.sum(jnp.where(mine, taps_k, 0.0), axis=0, keepdims=True)
            here = pltpu.roll(jnp.broadcast_to(taps_k, (tok, tok)), 0, 1, stride=1, stride_axis=0)
        else:
            here = jnp.zeros((tok, tok), F32)
        g_ref[k * tok : (k + 1) * tok, :] = jnp.where(upper, here, before).astype(BF)
        before = here
    for k in range(1, lags):
        z_ref[0 : k * gsize, k * tok : (k + 1) * tok] = jnp.zeros((k * gsize, tok), BF)
    lane = lax.broadcasted_iota(jnp.int32, (chunk, gsize, tok), 2)
    for a in range(0, blocks, chunk):
        conved = []
        for p in range(3):
            rows = slice(p * gsize, (p + 1) * gsize)
            if a == 0:
                now = x_ref[0:chunk, rows, :].astype(F32)
                slab = jnp.concatenate([jnp.zeros((1, gsize, tok), F32), now], axis=0)
            else:
                slab = x_ref[a - 1 : a + chunk, rows, :].astype(F32)
            total = coef[p][0] * slab[1:]
            flat = slab.reshape((chunk + 1) * gsize, tok)
            for d in range(1, taps):
                turned = pltpu.roll(flat, d, 1).reshape(chunk + 1, gsize, tok)
                total = total + coef[p][d] * jnp.where(lane < d, turned[:chunk], turned[1:])
            conved.append(total)
        gate_ref[a * gsize : (a + chunk) * gsize, :] = conved[0].reshape(chunk * gsize, tok)
        values = (conved[1] * conved[2]).reshape(chunk * gsize, tok).astype(BF)
        for k in range(lags):
            first = (a + k) * gsize
            count = min(chunk * gsize, blocks * gsize - first)
            if count > 0:
                z_ref[first : first + count, k * tok : (k + 1) * tok] = values[:count]
    mixed = jnp.dot(z_ref[...], g_ref[...], preferred_element_type=F32)
    out_ref[...] = (gate_ref[...] * mixed).astype(BF).reshape(blocks, gsize, tok)
    w_copy.wait()


FIRST = ((1, 0), (3, 0), (2, 1), (3, 1))
LAST = ((0, 0), (2, 0), (0, 1), (1, 1))


def products(ht, w_ref, pieces, own):
    tp = lax.axis_index("tp")
    y = lax.div(tp, 2)
    core = lax.rem(tp, 2)
    if not own:
        core = 1 - core
    half = w_ref.shape[1] // 16
    y1 = jnp.bitwise_xor(y, 1)
    order = (y, y1, 3 - y, 3 - y1)
    for slot, (q, side) in enumerate(pieces):
        start = pl.multiple_of((order[q] * 2 + core) * (2 * half) + side * half, half)
        yield slot, jnp.dot(ht, w_ref[:, pl.ds(start, half)], preferred_element_type=F32).astype(BF)


def project_first_kernel(h_ref, w_ref, out_ref, ht_ref):
    ht_ref[...] = h_ref[...].T
    for slot, piece in products(ht_ref[...], w_ref, FIRST, False):
        out_ref[slot] = piece


def project_kernel(ht_ref, w_ref, out_ref, *, pieces, own):
    for slot, piece in products(ht_ref[...], w_ref, pieces, own):
        out_ref[slot] = piece


def join_kernel(got_ref, own_ref, ht_in_ref, left_ref, right_ref, ht_ref):
    ht_ref[...] = ht_in_ref[...]
    total = got_ref[...].astype(F32) + own_ref[...].astype(F32)
    left_ref[...] = total[:2].astype(BF)
    right_ref[...] = total[2:].astype(BF)


def pass_kernel(got_ref, own_ref, left_in, right_in, left_out, right_out, left_kept, right_kept):
    total = got_ref[...].astype(F32) + own_ref[...].astype(F32)
    left_out[...] = (total[1] + left_in[1].astype(F32)).astype(BF)
    right_out[...] = (total[3] + right_in[1].astype(F32)).astype(BF)
    left_kept[...] = total[0] + left_in[0].astype(F32)
    right_kept[...] = total[2] + right_in[0].astype(F32)


def finish_kernel(left_kept, right_kept, left_in, right_in, out_ref):
    half = left_in.shape[1]
    out_ref[:, :half] = (left_kept[...] + left_in[...].astype(F32)).astype(BF)
    out_ref[:, half:] = (right_kept[...] + right_in[...].astype(F32)).astype(BF)


def body(projected, short_filter, long_filter, out_weight):
    tok, feats, channels = projected.shape
    groups, reach = long_filter.shape
    gsize = channels // groups
    dout = out_weight.shape[1]
    n_tp = lax.axis_size("tp")
    half = dout // n_tp // 2
    blocks = lax.axis_size("ctx")
    lags = reach // tok + 1

    short_filter = in_hbm(short_filter.transpose(1, 0, 2))
    packed, short_filter, long_filter = call(
        functools.partial(pack_kernel, gsize=gsize),
        [shaped((groups, feats * gsize, tok)), shaped(short_filter.shape, F32), shaped(long_filter.shape)],
        [HBM] * 3,
        scratch=(pltpu.VMEM((feats, tok, channels), BF), pltpu.SemaphoreType.DMA((feats + 2,))),
        limit=16,
    )(in_hbm(projected.transpose(1, 0, 2)), short_filter, in_hbm(long_filter))
    spread = lax.all_to_all(packed, "ctx", 0, 0, tiled=True)
    hidden, out_weight = call(
        functools.partial(conv_kernel, gsize=gsize, chunk=4),
        [shaped((blocks, gsize, tok)), shaped(out_weight.shape)],
        [VMEM] * 3 + [HBM],
        scratch=(
            pltpu.VMEM((blocks * gsize, lags * tok), BF),
            pltpu.VMEM((lags * tok, tok), BF),
            pltpu.VMEM((blocks * gsize, tok), F32),
            pltpu.SemaphoreType.DMA,
        ),
        limit=24,
    )(spread, short_filter, long_filter, in_hbm(out_weight))
    hidden = lax.all_to_all(hidden, "ctx", 0, 0, tiled=True).reshape(channels, tok)

    def project(ht, pieces, own):
        return call(
            functools.partial(project_kernel, pieces=pieces, own=own),
            shaped((4, tok, half)),
            [VMEM] * 2,
            flops=8 * tok * channels * half,
            nbytes=8 * channels * half,
        )(ht, out_weight)

    def swap(x, peer):
        return lax.ppermute(x, "tp", [(i, peer(i)) for i in range(n_tp)])

    def near(i):
        return i ^ 2

    def far(i):
        return (3 - i // 2) * 2 + i % 2

    def partner(i):
        return i ^ 1

    piece = (tok, half)
    theirs, ht = call(
        project_first_kernel, [shaped((4,) + piece), shaped((tok, channels))], [VMEM] * 2
    )(hidden, out_weight)
    got = swap(theirs, partner)
    own = project(ht, FIRST, True)
    left, right, ht = call(
        join_kernel, [shaped((2,) + piece), shaped((2,) + piece), shaped((tok, channels))], [VMEM] * 3
    )(got, own, ht)
    left_in = swap(left, near)
    right_in = swap(right, far)
    theirs = project(ht, LAST, False)
    got = swap(theirs, partner)
    own = project(ht, LAST, True)
    left, right, left_kept, right_kept = call(
        pass_kernel, [shaped(piece), shaped(piece), shaped(piece, F32), shaped(piece, F32)], [VMEM] * 4
    )(got, own, left_in, right_in)
    left_in = swap(left, far)
    right_in = swap(right, near)
    return call(finish_kernel, shaped((tok, 2 * half)), [VMEM] * 4)(
        left_kept, right_kept, left_in, right_in
    )


def solution(mesh):
    return jax.shard_map(
        body,
        mesh=mesh,
        in_specs=(P("ctx", None, "tp"), P(None, None, "tp"), P("tp", None), P("tp", None)),
        out_specs=P("ctx", "tp"),
        check_vma=False,
    )
```

```python
import functools

import jax
import jax.numpy as jnp
from jax import lax
from jax.experimental import pallas as pl
from jax.experimental.pallas import tpu as pltpu
from jax.sharding import PartitionSpec as P

BF = jnp.bfloat16
F32 = jnp.float32
VMEM = pl.BlockSpec(memory_space=pltpu.VMEM)
HBM = pl.BlockSpec(memory_space=pltpu.HBM)

EDGE = 8
CHUNKS = 2


def in_hbm(x):
    return pltpu.with_memory_space_constraint(x, pltpu.HBM)


def shaped(shape, dtype=BF):
    return jax.ShapeDtypeStruct(shape, dtype)


def call(kernel, out_shape, in_specs, scratch=(), limit=16, flops=0, nbytes=0):
    many = isinstance(out_shape, (list, tuple))
    return pl.pallas_call(
        kernel,
        out_shape=out_shape,
        in_specs=in_specs,
        out_specs=[VMEM] * len(out_shape) if many else VMEM,
        scratch_shapes=list(scratch),
        compiler_params=pltpu.CompilerParams(vmem_limit_bytes=limit << 20),
        cost_estimate=pl.CostEstimate(flops=flops, bytes_accessed=nbytes, transcendentals=0),
    )


def short_conv(x, sf_ref, feature, lanes):
    total = sf_ref[feature, 0:1, lanes] * x
    for d in range(1, sf_ref.shape[1]):
        total = total + sf_ref[feature, d : d + 1, lanes] * pltpu.roll(x, d, 0)
    return total


def pack_kernel(x_hbm, sf_hbm, out_ref, x_ref, sf_ref, sems, *, gsize):
    feats, tokens, channels = x_hbm.shape
    copies = [pltpu.make_async_copy(sf_hbm, sf_ref, sems.at[feats])]
    copies += [pltpu.make_async_copy(x_hbm.at[f], x_ref.at[f], sems.at[f]) for f in range(feats)]
    for copy in copies:
        copy.start()
    for copy in copies:
        copy.wait()
    pad = jnp.zeros((64 - 2 * EDGE * feats, 128), F32)
    left = lax.broadcasted_iota(jnp.int32, (128 // gsize, 8, 128), 2) < 64
    for j in range(0, channels, 128):
        lanes = slice(j, j + 128)
        groups = slice(j // gsize, (j + 128) // gsize)
        x = [x_ref[f, :, lanes].astype(F32) for f in range(feats)]
        values = short_conv(x[1], sf_ref, 1, lanes) * short_conv(x[2], sf_ref, 2, lanes)
        out_ref[groups, :gsize, :] = values.T.astype(BF).reshape(128 // gsize, gsize, tokens)
        edges = []
        for f in range(feats):
            edges += [x[f][tokens - EDGE :], x[f][:EDGE]]
        edges = jnp.concatenate((edges + [pad]) * 2, axis=0).T.reshape(128 // gsize, gsize, 128)
        out_ref[groups, gsize:, :] = jnp.where(left, edges[:, :8], edges[:, 8:]).astype(BF)


def prep_kernel(x_hbm, sf_hbm, lf_hbm, g_ref, gate_ref, coef_ref, x_ref, sf_ref, lf_ref, sems, *, gsize):
    tok, channels = x_ref.shape
    _, taps, _ = sf_ref.shape
    groups, reach = lf_ref.shape
    lags = reach // tok + 1
    copies = [
        pltpu.make_async_copy(sf_hbm, sf_ref, sems.at[0]),
        pltpu.make_async_copy(lf_hbm, lf_ref, sems.at[1]),
        pltpu.make_async_copy(x_hbm.at[0], x_ref, sems.at[2]),
    ]
    for copy in copies:
        copy.start()
    me = lax.axis_index("ctx")
    for copy in copies:
        copy.wait()
    row = lax.broadcasted_iota(jnp.int32, (8, channels), 0)
    col = lax.broadcasted_iota(jnp.int32, (8, channels), 1)
    lane = lax.broadcasted_iota(jnp.int32, (8, 128), 1)
    for d in range(taps):
        tile = jnp.zeros((8, 128), F32)
        for h in range(2):
            pick = col == row + (me * gsize + 8 * h)
            for f in range(3):
                tap = jnp.sum(jnp.where(pick, sf_ref[f, d : d + 1, :], 0.0), axis=1, keepdims=True)
                tile = jnp.where(lane // 16 == 4 * h + f, jnp.broadcast_to(tap, (8, 128)), tile)
        coef_ref[d] = tile
    s_i = lax.broadcasted_iota(jnp.int32, (tok, tok), 0)
    t_i = lax.broadcasted_iota(jnp.int32, (tok, tok), 1)
    upper = t_i >= s_i
    mine = lax.broadcasted_iota(jnp.int32, (groups, tok), 0) == me
    before = jnp.zeros((tok, tok), F32)
    for k in range(lags):
        if k < lags - 1:
            taps_k = lf_ref[:, k * tok : (k + 1) * tok].astype(F32)
            taps_k = jnp.sum(jnp.where(mine, taps_k, 0.0), axis=0, keepdims=True)
            here = pltpu.roll(jnp.broadcast_to(taps_k, (tok, tok)), 0, 1, stride=1, stride_axis=0)
        else:
            here = jnp.zeros((tok, tok), F32)
        g_ref[k * tok : (k + 1) * tok, :] = jnp.where(upper, here, before).astype(BF)
        before = here
    for j in range(0, channels, 128):
        lanes = slice(j, j + 128)
        gate_ref[:, lanes] = short_conv(x_ref[:, lanes].astype(F32), sf_ref, 0, lanes)


def blocks_of(first, own):
    tp = lax.axis_index("tp")
    y = lax.div(tp, 2)
    core = lax.rem(tp, 2)
    if not own:
        core = 1 - core
    near = jnp.bitwise_xor(y, 1)
    far = 3 - y
    even = core == 0
    if first:
        chips = (jnp.where(even, near, far), 3 - near)
    else:
        chips = (y, jnp.where(even, far, near))
    return [chip * 2 + core for chip in chips]


def fetches(w_hbm, w_ref, sems, wanted):
    cols = w_ref.shape[2]
    copies = []
    for slot, block in enumerate(wanted):
        start = pl.multiple_of(block * cols, cols)
        copies.append(pltpu.make_async_copy(w_hbm.at[:, pl.ds(start, cols)], w_ref.at[slot], sems.at[slot]))
    for copy in copies:
        copy.start()
    return copies


def conv_kernel(x_ref, g_ref, coef_ref, w_hbm, out_ref, w_ref, z_ref, sems, *, gsize):
    copies = fetches(w_hbm, w_ref, sems, blocks_of(True, False) + blocks_of(True, True))
    blocks, _, tok = x_ref.shape
    taps = coef_ref.shape[0]
    lags = g_ref.shape[0] // tok
    lane = lax.broadcasted_iota(jnp.int32, (blocks, 8, tok), 2)
    edge = x_ref[:, gsize:, :].astype(F32)
    before = jnp.concatenate([jnp.zeros((1, 8, tok), F32), edge[:-1]], axis=0)
    edge = jnp.where(lane % (2 * EDGE) < EDGE, before, edge).reshape(blocks * 8, tok)
    conved = jnp.zeros((blocks, 8, tok), F32)
    for d in range(taps):
        turned = edge if d == 0 else pltpu.roll(edge, d, 1)
        conved = conved + coef_ref[d][None] * turned.reshape(blocks, 8, tok)
    conved = conved.reshape(blocks * 8, tok)

    def at(first):
        return pltpu.roll(conved, tok - first, 1).reshape(blocks, 8, tok)

    gate = jnp.concatenate([at(EDGE), at(64 + EDGE)], axis=1)
    key = jnp.concatenate([at(3 * EDGE), at(64 + 3 * EDGE)], axis=1)
    value = jnp.concatenate([at(5 * EDGE), at(64 + 5 * EDGE)], axis=1)
    head = lax.broadcasted_iota(jnp.int32, (blocks, gsize, tok), 2) < EDGE
    values = jnp.where(head, key * value, x_ref[:, :gsize, :].astype(F32))
    values = values.astype(BF).reshape(blocks * gsize, tok)
    for k in range(lags):
        if k:
            z_ref[0 : k * gsize, k * tok : (k + 1) * tok] = jnp.zeros((k * gsize, tok), BF)
        z_ref[k * gsize :, k * tok : (k + 1) * tok] = values[: (blocks - k) * gsize]
    mixed = jnp.dot(z_ref[...], g_ref[...], preferred_element_type=F32).reshape(blocks, gsize, tok)
    out_ref[...] = jnp.where(head, gate * mixed, mixed).astype(BF)
    for copy in copies:
        copy.wait()


def product(ht, weight):
    return jnp.dot(ht, weight, preferred_element_type=F32).astype(BF)


def first_theirs_kernel(h_ref, gate_ref, w_ref, out_ref, ht_ref):
    mixed = h_ref[...].T
    ht_ref[...] = (gate_ref[...] * mixed.astype(F32)).astype(BF)
    ht_ref[:EDGE, :] = mixed[:EDGE]
    for slot in range(2):
        out_ref[slot] = product(ht_ref[...], w_ref[slot])


def first_own_kernel(ht_ref, w_ref, out_ref):
    for slot in range(2):
        out_ref[slot] = product(ht_ref[...], w_ref[slot + 2])


def last_kernel(ht_ref, w_hbm, out_ref, w_ref, sems, *, own):
    copies = fetches(w_hbm, w_ref, sems, blocks_of(False, own))
    for slot in range(2):
        copies[slot].wait()
        out_ref[slot] = product(ht_ref[...], w_ref[slot])


def join_kernel(got_ref, own_ref, ht_in_ref, *refs):
    *out_refs, ht_ref = refs
    ht_ref[...] = ht_in_ref[...]
    width = out_refs[0].shape[2]
    for i, out_ref in enumerate(out_refs):
        lanes = slice(i * width, (i + 1) * width)
        out_ref[...] = (got_ref[:, :, lanes].astype(F32) + own_ref[:, :, lanes].astype(F32)).astype(BF)


def pass_kernel(got_ref, own_ref, in_ref, *refs, chunk):
    out_ref, kept_ref = refs[-2:]
    width = in_ref.shape[2]
    lanes = slice(chunk * width, (chunk + 1) * width)
    total = got_ref[:, :, lanes].astype(F32) + own_ref[:, :, lanes].astype(F32) + in_ref[...].astype(F32)
    kept_ref[...] = total[0]
    out_ref[...] = total[1].astype(BF)


def finish_kernel(*refs):
    *in_refs, out_ref = refs
    count = len(in_refs) // 2
    width = in_refs[0].shape[1]
    for i in range(count):
        out_ref[:, i * width : (i + 1) * width] = (in_refs[i][...] + in_refs[count + i][...].astype(F32)).astype(BF)


def body(projected, short_filter, long_filter, out_weight):
    tok, feats, channels = projected.shape
    groups, reach = long_filter.shape
    gsize = channels // groups
    taps = short_filter.shape[0]
    dout = out_weight.shape[1]
    n_tp = lax.axis_size("tp")
    cols = dout // n_tp
    blocks = lax.axis_size("ctx")
    lags = reach // tok + 1

    x = in_hbm(projected.transpose(1, 0, 2))
    sf = in_hbm(short_filter.transpose(1, 0, 2))
    packed = call(
        functools.partial(pack_kernel, gsize=gsize),
        shaped((groups, gsize + 8, tok)),
        [HBM] * 2,
        scratch=(
            pltpu.VMEM((feats, tok, channels), BF),
            pltpu.VMEM((feats, taps, channels), F32),
            pltpu.SemaphoreType.DMA((feats + 1,)),
        ),
    )(x, sf)
    spread = lax.all_to_all(packed, "ctx", 0, 0, tiled=True)
    toeplitz, gate, coef = call(
        functools.partial(prep_kernel, gsize=gsize),
        [
            shaped((lags * tok, tok)),
            shaped((tok, channels), F32),
            shaped((taps, 8, 128), F32),
        ],
        [HBM] * 3,
        scratch=(
            pltpu.VMEM((tok, channels), BF),
            pltpu.VMEM((feats, taps, channels), F32),
            pltpu.VMEM(long_filter.shape, BF),
            pltpu.SemaphoreType.DMA((3,)),
        ),
    )(x, sf, in_hbm(long_filter))
    weight = in_hbm(out_weight)
    mixed, first_weight = call(
        functools.partial(conv_kernel, gsize=gsize),
        [shaped((blocks, gsize, tok)), shaped((4, channels, cols))],
        [VMEM] * 3 + [HBM],
        scratch=(pltpu.VMEM((blocks * gsize, lags * tok), BF), pltpu.SemaphoreType.DMA((4,))),
    )(spread, toeplitz, coef, weight)
    mixed = lax.all_to_all(mixed, "ctx", 0, 0, tiled=True).reshape(channels, tok)

    def project_last(ht, own):
        return call(
            functools.partial(last_kernel, own=own),
            shaped((2, tok, cols)),
            [VMEM, HBM],
            scratch=(pltpu.VMEM((2, channels, cols), BF), pltpu.SemaphoreType.DMA((2,))),
            flops=4 * tok * channels * cols,
            nbytes=4 * channels * cols,
        )(ht, weight)

    def swap(x, peer):
        return lax.ppermute(x, "tp", [(i, peer(i)) for i in range(n_tp)])

    def partner(i):
        return i ^ 1

    def hop_one(i):
        return i ^ 2 if i % 2 == 0 else 8 - i

    def hop_two(i):
        return 6 - i if i % 2 == 0 else i ^ 2

    width = cols // CHUNKS
    theirs, ht = call(
        first_theirs_kernel, [shaped((2, tok, cols)), shaped((tok, channels))], [VMEM] * 3
    )(mixed, gate, first_weight)
    got = swap(theirs, partner)
    own = call(first_own_kernel, shaped((2, tok, cols)), [VMEM] * 2)(ht, first_weight)
    *sends, ht = call(
        join_kernel, [shaped((2, tok, width))] * CHUNKS + [shaped((tok, channels))], [VMEM] * 3
    )(got, own, ht)
    arrived = []
    for i in range(CHUNKS):
        arrived.append(swap(sends[i], hop_one))
    theirs = project_last(ht, False)
    got = swap(theirs, partner)
    own = project_last(ht, True)
    kept, last = [], []
    for i in range(CHUNKS):
        onward, keep = call(
            functools.partial(pass_kernel, chunk=i),
            [shaped((tok, width)), shaped((tok, width), F32)],
            [VMEM] * (3 + min(i, 1)),
        )(got, own, arrived[i], *kept[-1:])
        kept.append(keep)
        last.append(swap(onward, hop_two))
    return call(finish_kernel, shaped((tok, cols)), [VMEM] * (2 * CHUNKS))(*kept, *last)


def solution(mesh):
    return jax.shard_map(
        body,
        mesh=mesh,
        in_specs=(P("ctx", None, "tp"), P(None, None, "tp"), P("tp", None), P("tp", None)),
        out_specs=P("ctx", "tp"),
        check_vma=False,
    )
```

```python
import functools

import jax
import jax.numpy as jnp
from jax import lax
from jax.experimental import pallas as pl
from jax.experimental.pallas import tpu as pltpu
from jax.sharding import PartitionSpec as P

BF = jnp.bfloat16
F32 = jnp.float32
VMEM = pl.BlockSpec(memory_space=pltpu.VMEM)
HBM = pl.BlockSpec(memory_space=pltpu.HBM)

EDGE = 8
SPLIT = (0, 768, 1024)
CHUNKS = len(SPLIT) - 1


def in_hbm(x):
    return pltpu.with_memory_space_constraint(x, pltpu.HBM)


def shaped(shape, dtype=BF):
    return jax.ShapeDtypeStruct(shape, dtype)


def call(kernel, out_shape, in_specs, scratch=(), limit=16, flops=0, nbytes=0, out_specs=None):
    many = isinstance(out_shape, (list, tuple))
    return pl.pallas_call(
        kernel,
        out_shape=out_shape,
        in_specs=in_specs,
        out_specs=out_specs or ([VMEM] * len(out_shape) if many else VMEM),
        scratch_shapes=list(scratch),
        compiler_params=pltpu.CompilerParams(vmem_limit_bytes=limit << 20),
        cost_estimate=pl.CostEstimate(flops=flops, bytes_accessed=nbytes, transcendentals=0),
    )


def short_conv(x, sf_ref, feature, lanes):
    total = sf_ref[feature, 0:1, lanes] * x
    for d in range(1, sf_ref.shape[1]):
        total = total + sf_ref[feature, d : d + 1, lanes] * pltpu.roll(x, d, 0)
    return total


def pack_kernel(x_hbm, sf_hbm, out_hbm, x_ref, head_ref, tail_ref, sf_ref, out_ref, sems, *, gsize):
    feats, tokens, channels = x_hbm.shape
    parts = channels // 128
    few = 128 // gsize
    firsts = [
        pltpu.make_async_copy(sf_hbm, sf_ref, sems.at[parts]),
        pltpu.make_async_copy(x_hbm.at[0, :EDGE], head_ref, sems.at[parts + 1]),
        pltpu.make_async_copy(x_hbm.at[0, tokens - EDGE :], tail_ref, sems.at[parts + 2]),
    ]
    reads = [
        pltpu.make_async_copy(
            x_hbm.at[1:, :, j * 128 : (j + 1) * 128], x_ref.at[:, :, j * 128 : (j + 1) * 128], sems.at[j]
        )
        for j in range(parts)
    ]
    writes = [
        pltpu.make_async_copy(
            out_ref.at[j * few : (j + 1) * few], out_hbm.at[j * few : (j + 1) * few], sems.at[parts + 3 + j]
        )
        for j in range(parts)
    ]
    for copy in firsts + reads:
        copy.start()
    for copy in firsts:
        copy.wait()
    pad = jnp.zeros((64 - 2 * EDGE * feats, 128), F32)
    left = lax.broadcasted_iota(jnp.int32, (few, 8, 128), 2) < 64
    for j in range(parts):
        lanes = slice(j * 128, (j + 1) * 128)
        groups = slice(j * few, (j + 1) * few)
        reads[j].wait()
        x = [x_ref[f, :, lanes].astype(F32) for f in range(feats - 1)]
        values = short_conv(x[0], sf_ref, 1, lanes) * short_conv(x[1], sf_ref, 2, lanes)
        out_ref[groups, :gsize, :] = values.T.astype(BF).reshape(few, gsize, tokens)
        edges = [tail_ref[:, lanes].astype(F32), head_ref[:, lanes].astype(F32)]
        for f in range(feats - 1):
            edges += [x[f][tokens - EDGE :], x[f][:EDGE]]
        edges = jnp.concatenate((edges + [pad]) * 2, axis=0).T.reshape(few, gsize, 128)
        out_ref[groups, gsize:, :] = jnp.where(left, edges[:, :8], edges[:, 8:]).astype(BF)
        writes[j].start()
    for copy in writes:
        copy.wait()


def prep_kernel(x_hbm, sf_hbm, lf_hbm, g_ref, gate_ref, coef_ref, x_ref, sf_ref, lf_ref, sems, *, gsize):
    tok, channels = x_ref.shape
    _, taps, _ = sf_ref.shape
    groups, reach = lf_ref.shape
    lags = reach // tok + 1
    copies = [
        pltpu.make_async_copy(sf_hbm, sf_ref, sems.at[0]),
        pltpu.make_async_copy(lf_hbm, lf_ref, sems.at[1]),
        pltpu.make_async_copy(x_hbm.at[0], x_ref, sems.at[2]),
    ]
    for copy in copies:
        copy.start()
    me = lax.axis_index("ctx")
    for copy in copies:
        copy.wait()
    row = lax.broadcasted_iota(jnp.int32, (8, channels), 0)
    col = lax.broadcasted_iota(jnp.int32, (8, channels), 1)
    lane = lax.broadcasted_iota(jnp.int32, (8, 128), 1)
    for d in range(taps):
        tile = jnp.zeros((8, 128), F32)
        for h in range(2):
            pick = col == row + (me * gsize + 8 * h)
            for f in range(3):
                tap = jnp.sum(jnp.where(pick, sf_ref[f, d : d + 1, :], 0.0), axis=1, keepdims=True)
                tile = jnp.where(lane // 16 == 4 * h + f, jnp.broadcast_to(tap, (8, 128)), tile)
        coef_ref[d] = tile
    s_i = lax.broadcasted_iota(jnp.int32, (tok, tok), 0)
    t_i = lax.broadcasted_iota(jnp.int32, (tok, tok), 1)
    upper = t_i >= s_i
    mine = lax.broadcasted_iota(jnp.int32, (groups, tok), 0) == me
    before = jnp.zeros((tok, tok), F32)
    for k in range(lags):
        if k < lags - 1:
            taps_k = lf_ref[:, k * tok : (k + 1) * tok].astype(F32)
            taps_k = jnp.sum(jnp.where(mine, taps_k, 0.0), axis=0, keepdims=True)
            here = pltpu.roll(jnp.broadcast_to(taps_k, (tok, tok)), 0, 1, stride=1, stride_axis=0)
        else:
            here = jnp.zeros((tok, tok), F32)
        block = jnp.where(upper, here, before).astype(BF)
        g_ref[k * tok : (k + 1) * tok, tok:] = block
        g_ref[(k + 1) * tok : (k + 2) * tok, :tok] = block
        before = here
    g_ref[:tok, :tok] = jnp.zeros((tok, tok), BF)
    g_ref[lags * tok :, tok:] = jnp.zeros((tok, tok), BF)
    for j in range(0, channels, 128):
        lanes = slice(j, j + 128)
        gate_ref[:, lanes] = short_conv(x_ref[:, lanes].astype(F32), sf_ref, 0, lanes)


def blocks_of(first, own):
    tp = lax.axis_index("tp")
    y = lax.div(tp, 2)
    core = lax.rem(tp, 2)
    if not own:
        core = 1 - core
    near = jnp.bitwise_xor(y, 1)
    far = 3 - y
    even = core == 0
    if first:
        chips = (jnp.where(even, near, far), 3 - near)
    else:
        chips = (y, jnp.where(even, far, near))
    return [chip * 2 + core for chip in chips]


def fetches(w_hbm, w_ref, sems, wanted):
    cols = w_ref.shape[2]
    copies = []
    for slot, block in enumerate(wanted):
        start = pl.multiple_of(block * cols, cols)
        copies.append(pltpu.make_async_copy(w_hbm.at[:, pl.ds(start, cols)], w_ref.at[slot], sems.at[slot]))
    for copy in copies:
        copy.start()
    return copies


def conv_kernel(x_ref, g_ref, coef_ref, w_hbm, out_ref, w_ref, z_ref, sems, *, gsize):
    copies = fetches(w_hbm, w_ref, sems, blocks_of(True, False) + blocks_of(True, True))
    blocks, _, tok = x_ref.shape
    taps = coef_ref.shape[0]
    lane = lax.broadcasted_iota(jnp.int32, (blocks, 8, tok), 2)
    edge = x_ref[:, gsize:, :].astype(F32)
    before = jnp.concatenate([jnp.zeros((1, 8, tok), F32), edge[:-1]], axis=0)
    edge = jnp.where(lane % (2 * EDGE) < EDGE, before, edge).reshape(blocks * 8, tok)
    conved = jnp.zeros((blocks, 8, tok), F32)
    for d in range(taps):
        turned = edge if d == 0 else pltpu.roll(edge, d, 1)
        conved = conved + coef_ref[d][None] * turned.reshape(blocks, 8, tok)
    conved = conved.reshape(blocks * 8, tok)

    def at(first):
        return pltpu.roll(conved, tok - first, 1).reshape(blocks, 8, tok)

    gate = jnp.concatenate([at(EDGE), at(64 + EDGE)], axis=1)
    key = jnp.concatenate([at(3 * EDGE), at(64 + 3 * EDGE)], axis=1)
    value = jnp.concatenate([at(5 * EDGE), at(64 + 5 * EDGE)], axis=1)
    head = lax.broadcasted_iota(jnp.int32, (blocks, gsize, tok), 2) < EDGE
    values = jnp.where(head, key * value, x_ref[:, :gsize, :].astype(F32))
    values = values.astype(BF).reshape(blocks // 2, 2, gsize, tok)
    rows = blocks // 2 * gsize
    for k in range(g_ref.shape[0] // tok):
        source = values[:, 1 - k % 2].reshape(rows, tok)
        skip = k // 2 * gsize
        if skip:
            z_ref[:skip, k * tok : (k + 1) * tok] = jnp.zeros((skip, tok), BF)
        z_ref[skip:, k * tok : (k + 1) * tok] = source[: rows - skip]
    mixed = jnp.dot(z_ref[...], g_ref[...], preferred_element_type=F32).reshape(blocks // 2, gsize, 2 * tok)
    mixed = jnp.stack([mixed[:, :, :tok], mixed[:, :, tok:]], axis=1).reshape(blocks, gsize, tok)
    out_ref[...] = jnp.where(head, gate * mixed, mixed).astype(BF)
    for copy in copies:
        copy.wait()


def product(ht, weight):
    return jnp.dot(ht, weight, preferred_element_type=F32).astype(BF)


def first_theirs_kernel(h_ref, gate_ref, w_ref, out_ref, ht_ref):
    mixed = h_ref[...].T
    ht_ref[...] = (gate_ref[...] * mixed.astype(F32)).astype(BF)
    ht_ref[:EDGE, :] = mixed[:EDGE]
    for slot in range(2):
        out_ref[slot] = product(ht_ref[...], w_ref[slot])


def first_own_kernel(ht_ref, w_ref, w_hbm, out_ref, last_ref, sems):
    copies = fetches(w_hbm, last_ref, sems, blocks_of(False, False) + blocks_of(False, True))
    for slot in range(2):
        out_ref[slot] = product(ht_ref[...], w_ref[slot + 2])
    for copy in copies:
        copy.wait()


def last_kernel(ht_ref, w_ref, out_ref, *, first):
    for slot in range(2):
        out_ref[slot] = product(ht_ref[...], w_ref[first + slot])


def join_kernel(got_ref, own_ref, ht_in_ref, out_ref, ht_ref, *, chunk):
    ht_ref[...] = ht_in_ref[...]
    lanes = slice(SPLIT[chunk], SPLIT[chunk + 1])
    out_ref[...] = (got_ref[:, :, lanes].astype(F32) + own_ref[:, :, lanes].astype(F32)).astype(BF)


def pass_kernel(got_ref, own_ref, in_ref, *refs, chunk):
    out_ref, kept_ref = refs[-2:]
    lanes = slice(SPLIT[chunk], SPLIT[chunk + 1])
    total = got_ref[:, :, lanes].astype(F32) + own_ref[:, :, lanes].astype(F32) + in_ref[...].astype(F32)
    kept_ref[...] = total[0]
    out_ref[...] = total[1].astype(BF)


def finish_kernel(*refs):
    *in_refs, out_ref = refs
    for i in range(CHUNKS):
        total = in_refs[i][...] + in_refs[CHUNKS + i][...].astype(F32)
        out_ref[:, SPLIT[i] : SPLIT[i + 1]] = total.astype(BF)


def body(projected, short_filter, long_filter, out_weight):
    tok, feats, channels = projected.shape
    groups, reach = long_filter.shape
    gsize = channels // groups
    taps = short_filter.shape[0]
    dout = out_weight.shape[1]
    n_tp = lax.axis_size("tp")
    cols = dout // n_tp
    blocks = lax.axis_size("ctx")
    lags = reach // tok + 1

    x = in_hbm(projected.transpose(1, 0, 2))
    sf = in_hbm(short_filter.transpose(1, 0, 2))
    packed = call(
        functools.partial(pack_kernel, gsize=gsize),
        shaped((groups, gsize + 8, tok)),
        [HBM] * 2,
        scratch=(
            pltpu.VMEM((feats - 1, tok, channels), BF),
            pltpu.VMEM((EDGE, channels), BF),
            pltpu.VMEM((EDGE, channels), BF),
            pltpu.VMEM((feats, taps, channels), F32),
            pltpu.VMEM((groups, gsize + 8, tok), BF),
            pltpu.SemaphoreType.DMA((2 * channels // 128 + 3,)),
        ),
        out_specs=HBM,
    )(x, sf)
    spread = lax.all_to_all(packed, "ctx", 0, 0, tiled=True)
    toeplitz, gate, coef = call(
        functools.partial(prep_kernel, gsize=gsize),
        [
            shaped(((lags + 1) * tok, 2 * tok)),
            shaped((tok, channels), F32),
            shaped((taps, 8, 128), F32),
        ],
        [HBM] * 3,
        scratch=(
            pltpu.VMEM((tok, channels), BF),
            pltpu.VMEM((feats, taps, channels), F32),
            pltpu.VMEM(long_filter.shape, BF),
            pltpu.SemaphoreType.DMA((3,)),
        ),
    )(x, sf, in_hbm(long_filter))
    weight = in_hbm(out_weight)
    mixed, first_weight = call(
        functools.partial(conv_kernel, gsize=gsize),
        [shaped((blocks, gsize, tok)), shaped((4, channels, cols))],
        [VMEM] * 3 + [HBM],
        scratch=(pltpu.VMEM((blocks // 2 * gsize, (lags + 1) * tok), BF), pltpu.SemaphoreType.DMA((4,))),
    )(spread, toeplitz, coef, weight)
    mixed = lax.all_to_all(mixed, "ctx", 0, 0, tiled=True).reshape(channels, tok)

    def project_last(ht, first):
        return call(
            functools.partial(last_kernel, first=first),
            shaped((2, tok, cols)),
            [VMEM] * 2,
            flops=4 * tok * channels * cols,
            nbytes=4 * channels * cols,
        )(ht, last_weight)

    def swap(x, peer):
        return lax.ppermute(x, "tp", [(i, peer(i)) for i in range(n_tp)])

    def partner(i):
        return i ^ 1

    def hop_one(i):
        return i ^ 2 if i % 2 == 0 else 8 - i

    def hop_two(i):
        return 6 - i if i % 2 == 0 else i ^ 2

    widths = [SPLIT[i + 1] - SPLIT[i] for i in range(CHUNKS)]
    theirs, ht = call(
        first_theirs_kernel, [shaped((2, tok, cols)), shaped((tok, channels))], [VMEM] * 3
    )(mixed, gate, first_weight)
    got = swap(theirs, partner)
    own, last_weight = call(
        first_own_kernel,
        [shaped((2, tok, cols)), shaped((4, channels, cols))],
        [VMEM] * 2 + [HBM],
        scratch=(pltpu.SemaphoreType.DMA((4,)),),
    )(ht, first_weight, weight)
    arrived = []
    for i in range(CHUNKS):
        send, ht = call(
            functools.partial(join_kernel, chunk=i), [shaped((2, tok, widths[i])), shaped((tok, channels))], [VMEM] * 3
        )(got, own, ht)
        arrived.append(swap(send, hop_one))
    theirs = project_last(ht, 0)
    got = swap(theirs, partner)
    own = project_last(ht, 2)
    kept, last = [], []
    for i in range(CHUNKS):
        onward, keep = call(
            functools.partial(pass_kernel, chunk=i),
            [shaped((tok, widths[i])), shaped((tok, widths[i]), F32)],
            [VMEM] * (3 + min(i, 1)),
        )(got, own, arrived[i], *kept[-1:])
        kept.append(keep)
        last.append(swap(onward, hop_two))
    return call(finish_kernel, shaped((tok, cols)), [VMEM] * (2 * CHUNKS))(*kept, *last)


def solution(mesh):
    return jax.shard_map(
        body,
        mesh=mesh,
        in_specs=(P("ctx", None, "tp"), P(None, None, "tp"), P("tp", None), P("tp", None)),
        out_specs=P("ctx", "tp"),
        check_vma=False,
    )
```

```python
import functools

import jax
import jax.numpy as jnp
from jax import lax
from jax.experimental import pallas as pl
from jax.experimental.pallas import tpu as pltpu
from jax.sharding import PartitionSpec as P

BF = jnp.bfloat16
F32 = jnp.float32
VMEM = pl.BlockSpec(memory_space=pltpu.VMEM)
HBM = pl.BlockSpec(memory_space=pltpu.HBM)

EDGE = 8
SPLIT = (0, 512, 1024)
CHUNKS = len(SPLIT) - 1


def in_hbm(x):
    return pltpu.with_memory_space_constraint(x, pltpu.HBM)


def shaped(shape, dtype=BF):
    return jax.ShapeDtypeStruct(shape, dtype)


def call(kernel, out_shape, in_specs, scratch=(), limit=16, flops=0, nbytes=0, out_specs=None):
    many = isinstance(out_shape, (list, tuple))
    return pl.pallas_call(
        kernel,
        out_shape=out_shape,
        in_specs=in_specs,
        out_specs=out_specs or ([VMEM] * len(out_shape) if many else VMEM),
        scratch_shapes=list(scratch),
        compiler_params=pltpu.CompilerParams(vmem_limit_bytes=limit << 20),
        cost_estimate=pl.CostEstimate(flops=flops, bytes_accessed=nbytes, transcendentals=0),
    )


def short_conv(x, sf_ref, feature, lanes):
    total = sf_ref[feature, 0:1, lanes] * x
    for d in range(1, sf_ref.shape[1]):
        total = total + sf_ref[feature, d : d + 1, lanes] * pltpu.roll(x, d, 0)
    return total


def short_conv_rows(x, rows_ref, sf_ref, feature, lanes):
    tokens = x.shape[0]
    rows_ref[:8, :] = jnp.zeros((8, x.shape[1]), F32)
    rows_ref[8:, :] = x
    total = sf_ref[feature, 0:1, lanes] * x
    for d in range(1, sf_ref.shape[1]):
        total = total + sf_ref[feature, d : d + 1, lanes] * rows_ref[8 - d : 8 - d + tokens, :]
    return total


def pack_kernel(x_hbm, sf_hbm, out_hbm, x_ref, head_ref, tail_ref, sf_ref, out_ref, rows_ref, sems, *, gsize):
    feats, tokens, channels = x_hbm.shape
    parts = channels // 128
    few = 128 // gsize
    firsts = [
        pltpu.make_async_copy(sf_hbm, sf_ref, sems.at[parts]),
        pltpu.make_async_copy(x_hbm.at[0, :EDGE], head_ref, sems.at[parts + 1]),
        pltpu.make_async_copy(x_hbm.at[0, tokens - EDGE :], tail_ref, sems.at[parts + 2]),
    ]
    reads = [
        pltpu.make_async_copy(
            x_hbm.at[1:, :, j * 128 : (j + 1) * 128], x_ref.at[:, :, j * 128 : (j + 1) * 128], sems.at[j]
        )
        for j in range(parts)
    ]
    writes = [
        pltpu.make_async_copy(
            out_ref.at[j * few : (j + 1) * few], out_hbm.at[j * few : (j + 1) * few], sems.at[parts + 3 + j]
        )
        for j in range(parts)
    ]
    for copy in firsts + reads:
        copy.start()
    for copy in firsts:
        copy.wait()
    pad = jnp.zeros((64 - 2 * EDGE * feats, 128), F32)
    left = lax.broadcasted_iota(jnp.int32, (few, 8, 128), 2) < 64
    for j in range(parts):
        lanes = slice(j * 128, (j + 1) * 128)
        groups = slice(j * few, (j + 1) * few)
        reads[j].wait()
        x = [x_ref[f, :, lanes].astype(F32) for f in range(feats - 1)]
        key = short_conv_rows(x[0], rows_ref.at[j, 0], sf_ref, 1, lanes)
        values = key * short_conv_rows(x[1], rows_ref.at[j, 1], sf_ref, 2, lanes)
        out_ref[groups, :gsize, :] = values.T.astype(BF).reshape(few, gsize, tokens)
        edges = [tail_ref[:, lanes].astype(F32), head_ref[:, lanes].astype(F32)]
        for f in range(feats - 1):
            edges += [x[f][tokens - EDGE :], x[f][:EDGE]]
        edges = jnp.concatenate((edges + [pad]) * 2, axis=0).T.reshape(few, gsize, 128)
        out_ref[groups, gsize:, :] = jnp.where(left, edges[:, :8], edges[:, 8:]).astype(BF)
        writes[j].start()
    for copy in writes:
        copy.wait()


def pieces_of(first, own):
    tp = lax.axis_index("tp")
    y = lax.div(tp, 2)
    core = lax.rem(tp, 2)
    if not own:
        core = 1 - core
    near = jnp.bitwise_xor(y, 1)
    far = 3 - y
    slots = []
    for slot in range(2):
        row = []
        for chunk in range(CHUNKS):
            even = lax.rem(core + chunk, 2) == 0
            if first:
                chip = jnp.where(even, near, far) if slot == 0 else 3 - near
            else:
                chip = y if slot == 0 else jnp.where(even, far, near)
            row.append(chip * 2 + core)
        slots.append(row)
    return slots


def fetches(w_hbm, w_ref, sems, wanted):
    cols = w_ref.shape[2]
    copies = []
    for slot, row in enumerate(wanted):
        for chunk, block in enumerate(row):
            low, high = SPLIT[chunk], SPLIT[chunk + 1]
            start = pl.multiple_of(block * cols + low, 128)
            copies.append(
                pltpu.make_async_copy(
                    w_hbm.at[:, pl.ds(start, high - low)],
                    w_ref.at[slot, :, low:high],
                    sems.at[slot * CHUNKS + chunk],
                )
            )
    for copy in copies:
        copy.start()
    return copies


def prep_kernel(
    x_hbm, sf_hbm, lf_hbm, w_hbm, g_ref, gate_ref, coef_ref, w_ref, x_ref, sf_ref, lf_ref, sems, w_sems, *, gsize
):
    tok, channels = x_ref.shape
    _, taps, _ = sf_ref.shape
    groups, reach = lf_ref.shape
    lags = reach // tok + 1
    copies = [
        pltpu.make_async_copy(sf_hbm, sf_ref, sems.at[0]),
        pltpu.make_async_copy(lf_hbm, lf_ref, sems.at[1]),
        pltpu.make_async_copy(x_hbm.at[0], x_ref, sems.at[2]),
    ]
    for copy in copies:
        copy.start()
    fetched = fetches(w_hbm, w_ref, w_sems, pieces_of(True, False))
    me = lax.axis_index("ctx")
    for copy in copies:
        copy.wait()
    row = lax.broadcasted_iota(jnp.int32, (8, channels), 0)
    col = lax.broadcasted_iota(jnp.int32, (8, channels), 1)
    lane = lax.broadcasted_iota(jnp.int32, (8, 128), 1)
    for d in range(taps):
        tile = jnp.zeros((8, 128), F32)
        for h in range(2):
            pick = col == row + (me * gsize + 8 * h)
            for f in range(3):
                tap = jnp.sum(jnp.where(pick, sf_ref[f, d : d + 1, :], 0.0), axis=1, keepdims=True)
                tile = jnp.where(lane // 16 == 4 * h + f, jnp.broadcast_to(tap, (8, 128)), tile)
        coef_ref[d] = tile
    s_i = lax.broadcasted_iota(jnp.int32, (tok, tok), 0)
    t_i = lax.broadcasted_iota(jnp.int32, (tok, tok), 1)
    upper = t_i >= s_i
    mine = lax.broadcasted_iota(jnp.int32, (groups, tok), 0) == me
    before = jnp.zeros((tok, tok), F32)
    for k in range(lags):
        if k < lags - 1:
            taps_k = lf_ref[:, k * tok : (k + 1) * tok].astype(F32)
            taps_k = jnp.sum(jnp.where(mine, taps_k, 0.0), axis=0, keepdims=True)
            here = pltpu.roll(jnp.broadcast_to(taps_k, (tok, tok)), 0, 1, stride=1, stride_axis=0)
        else:
            here = jnp.zeros((tok, tok), F32)
        g_ref[k * tok : (k + 1) * tok, :] = jnp.where(upper, here, before).astype(BF)
        before = here
    for j in range(0, channels, 128):
        lanes = slice(j, j + 128)
        gate_ref[:, lanes] = short_conv(x_ref[:, lanes].astype(F32), sf_ref, 0, lanes)
    for copy in fetched:
        copy.wait()


def conv_kernel(x_ref, t_ref, coef_ref, w_hbm, out_ref, w_ref, z_ref, g_ref, sems, *, gsize):
    copies = fetches(w_hbm, w_ref, sems, pieces_of(True, True)[:1])
    blocks, _, tok = x_ref.shape
    taps = coef_ref.shape[0]
    lane = lax.broadcasted_iota(jnp.int32, (blocks, 8, tok), 2)
    edge = x_ref[:, gsize:, :].astype(F32)
    before = jnp.concatenate([jnp.zeros((1, 8, tok), F32), edge[:-1]], axis=0)
    edge = jnp.where(lane % (2 * EDGE) < EDGE, before, edge).reshape(blocks * 8, tok)
    conved = jnp.zeros((blocks, 8, tok), F32)
    for d in range(taps):
        turned = edge if d == 0 else pltpu.roll(edge, d, 1)
        conved = conved + coef_ref[d][None] * turned.reshape(blocks, 8, tok)
    conved = conved.reshape(blocks * 8, tok)

    def at(first):
        return pltpu.roll(conved, tok - first, 1).reshape(blocks, 8, tok)

    gate = jnp.concatenate([at(EDGE), at(64 + EDGE)], axis=1)
    key = jnp.concatenate([at(3 * EDGE), at(64 + 3 * EDGE)], axis=1)
    value = jnp.concatenate([at(5 * EDGE), at(64 + 5 * EDGE)], axis=1)
    head = lax.broadcasted_iota(jnp.int32, (blocks, gsize, tok), 2) < EDGE
    values = jnp.where(head, key * value, x_ref[:, :gsize, :].astype(F32))
    g_ref[:tok, :tok] = jnp.zeros((tok, tok), BF)
    g_ref[tok:, :tok] = t_ref[...]
    g_ref[: t_ref.shape[0], tok:] = t_ref[...]
    g_ref[t_ref.shape[0] :, tok:] = jnp.zeros((tok, tok), BF)
    values = values.astype(BF).reshape(blocks // 2, 2, gsize, tok)
    rows = blocks // 2 * gsize
    for k in range(g_ref.shape[0] // tok):
        source = values[:, 1 - k % 2].reshape(rows, tok)
        skip = k // 2 * gsize
        if skip:
            z_ref[:skip, k * tok : (k + 1) * tok] = jnp.zeros((skip, tok), BF)
        z_ref[skip:, k * tok : (k + 1) * tok] = source[: rows - skip]
    mixed = jnp.dot(z_ref[...], g_ref[...], preferred_element_type=F32).reshape(blocks // 2, gsize, 2 * tok)
    mixed = jnp.stack([mixed[:, :, :tok], mixed[:, :, tok:]], axis=1).reshape(blocks, gsize, tok)
    out_ref[...] = jnp.where(head, gate * mixed, mixed).astype(BF)
    for copy in copies:
        copy.wait()


def product(ht, weight):
    return jnp.dot(ht, weight, preferred_element_type=F32).astype(BF)


def first_theirs_kernel(h_ref, gate_ref, w_ref, out_ref, ht_ref):
    mixed = h_ref[...].T
    ht_ref[...] = (gate_ref[...] * mixed.astype(F32)).astype(BF)
    ht_ref[:EDGE, :] = mixed[:EDGE]
    for slot in range(2):
        out_ref[slot] = product(ht_ref[...], w_ref[slot])


def first_own_kernel(ht_ref, w_ref, w_hbm, out_ref, rest_ref, sems):
    copies = fetches(w_hbm, rest_ref, sems, pieces_of(True, True)[1:])
    out_ref[0] = product(ht_ref[...], w_ref[0])
    for copy in copies:
        copy.wait()
    out_ref[1] = product(ht_ref[...], rest_ref[0])


def last_kernel(ht_ref, w_hbm, out_ref, w_ref, sems, *, own):
    copies = fetches(w_hbm, w_ref, sems, pieces_of(False, own))
    for slot in range(2):
        for copy in copies[slot * CHUNKS : (slot + 1) * CHUNKS]:
            copy.wait()
        out_ref[slot] = product(ht_ref[...], w_ref[slot])


def join_kernel(got_ref, own_ref, ht_in_ref, out_ref, ht_ref, *, chunk):
    ht_ref[...] = ht_in_ref[...]
    lanes = slice(SPLIT[chunk], SPLIT[chunk + 1])
    out_ref[...] = (got_ref[:, :, lanes].astype(F32) + own_ref[:, :, lanes].astype(F32)).astype(BF)


def pass_kernel(got_ref, own_ref, in_ref, *refs, chunk):
    out_ref, kept_ref = refs[-2:]
    lanes = slice(SPLIT[chunk], SPLIT[chunk + 1])
    total = got_ref[:, :, lanes].astype(F32) + own_ref[:, :, lanes].astype(F32) + in_ref[...].astype(F32)
    kept_ref[...] = total[0]
    out_ref[...] = total[1].astype(BF)


def finish_kernel(*refs):
    *in_refs, out_ref = refs
    for i in range(CHUNKS):
        total = in_refs[i][...] + in_refs[CHUNKS + i][...].astype(F32)
        out_ref[:, SPLIT[i] : SPLIT[i + 1]] = total.astype(BF)


def body(projected, short_filter, long_filter, out_weight):
    tok, feats, channels = projected.shape
    groups, reach = long_filter.shape
    gsize = channels // groups
    taps = short_filter.shape[0]
    dout = out_weight.shape[1]
    n_tp = lax.axis_size("tp")
    cols = dout // n_tp
    blocks = lax.axis_size("ctx")
    lags = reach // tok + 1

    x = in_hbm(projected.transpose(1, 0, 2))
    sf = in_hbm(short_filter.transpose(1, 0, 2))
    weight = in_hbm(out_weight)
    packed = call(
        functools.partial(pack_kernel, gsize=gsize),
        shaped((groups, gsize + 8, tok)),
        [HBM] * 2,
        scratch=(
            pltpu.VMEM((feats - 1, tok, channels), BF),
            pltpu.VMEM((EDGE, channels), BF),
            pltpu.VMEM((EDGE, channels), BF),
            pltpu.VMEM((feats, taps, channels), F32),
            pltpu.VMEM((groups, gsize + 8, tok), BF),
            pltpu.VMEM((channels // 128, feats - 1, tok + 8, 128), F32),
            pltpu.SemaphoreType.DMA((2 * channels // 128 + 3,)),
        ),
        out_specs=HBM,
    )(x, sf)
    spread = lax.all_to_all(packed, "ctx", 0, 0, tiled=True)
    toeplitz, gate, coef, theirs_weight = call(
        functools.partial(prep_kernel, gsize=gsize),
        [
            shaped((lags * tok, tok)),
            shaped((tok, channels), F32),
            shaped((taps, 8, 128), F32),
            shaped((2, channels, cols)),
        ],
        [HBM] * 4,
        scratch=(
            pltpu.VMEM((tok, channels), BF),
            pltpu.VMEM((feats, taps, channels), F32),
            pltpu.VMEM(long_filter.shape, BF),
            pltpu.SemaphoreType.DMA((3,)),
            pltpu.SemaphoreType.DMA((2 * CHUNKS,)),
        ),
    )(x, sf, in_hbm(long_filter), weight)
    mixed, own_weight = call(
        functools.partial(conv_kernel, gsize=gsize),
        [shaped((blocks, gsize, tok)), shaped((1, channels, cols))],
        [VMEM] * 3 + [HBM],
        scratch=(
            pltpu.VMEM((blocks // 2 * gsize, (lags + 1) * tok), BF),
            pltpu.VMEM(((lags + 1) * tok, 2 * tok), BF),
            pltpu.SemaphoreType.DMA((CHUNKS,)),
        ),
    )(spread, toeplitz, coef, weight)
    mixed = lax.all_to_all(mixed, "ctx", 0, 0, tiled=True).reshape(channels, tok)

    def project_last(ht, own):
        return call(
            functools.partial(last_kernel, own=own),
            shaped((2, tok, cols)),
            [VMEM, HBM],
            scratch=(pltpu.VMEM((2, channels, cols), BF), pltpu.SemaphoreType.DMA((2 * CHUNKS,))),
            flops=4 * tok * channels * cols,
            nbytes=4 * channels * cols,
        )(ht, weight)

    def swap(x, peer):
        return lax.ppermute(x, "tp", [(i, peer(i)) for i in range(n_tp)])

    def partner(i):
        return i ^ 1

    def hop(i, parity):
        return i ^ 2 if (i + parity) % 2 == 0 else (3 - i // 2) * 2 + i % 2

    widths = [SPLIT[i + 1] - SPLIT[i] for i in range(CHUNKS)]
    theirs, ht = call(
        first_theirs_kernel, [shaped((2, tok, cols)), shaped((tok, channels))], [VMEM] * 3
    )(mixed, gate, theirs_weight)
    got = swap(theirs, partner)
    own = call(
        first_own_kernel,
        shaped((2, tok, cols)),
        [VMEM] * 2 + [HBM],
        scratch=(pltpu.VMEM((1, channels, cols), BF), pltpu.SemaphoreType.DMA((CHUNKS,))),
    )(ht, own_weight, weight)
    arrived = []
    for i in range(CHUNKS):
        send, ht = call(
            functools.partial(join_kernel, chunk=i),
            [shaped((2, tok, widths[i])), shaped((tok, channels))],
            [VMEM] * 3,
        )(got, own, ht)
        arrived.append(swap(send, functools.partial(hop, parity=i)))
    theirs = project_last(ht, False)
    got = swap(theirs, partner)
    own = project_last(ht, True)
    kept, last = [], []
    for i in range(CHUNKS):
        onward, keep = call(
            functools.partial(pass_kernel, chunk=i),
            [shaped((tok, widths[i])), shaped((tok, widths[i]), F32)],
            [VMEM] * (3 + min(i, 1)),
        )(got, own, arrived[i], *kept[-1:])
        kept.append(keep)
        last.append(swap(onward, functools.partial(hop, parity=i + 1)))
    return call(finish_kernel, shaped((tok, cols)), [VMEM] * (2 * CHUNKS))(*kept, *last)


def solution(mesh):
    return jax.shard_map(
        body,
        mesh=mesh,
        in_specs=(P("ctx", None, "tp"), P(None, None, "tp"), P("tp", None), P("tp", None)),
        out_specs=P("ctx", "tp"),
        check_vma=False,
    )
```

```python
import functools

import jax
import jax.numpy as jnp
from jax import lax
from jax.experimental import pallas as pl
from jax.experimental.pallas import tpu as pltpu
from jax.sharding import PartitionSpec as P

BF = jnp.bfloat16
F32 = jnp.float32
VMEM = pl.BlockSpec(memory_space=pltpu.VMEM)
HBM = pl.BlockSpec(memory_space=pltpu.HBM)

EDGE = 8
SPLIT = (0, 640, 1024)
CHUNKS = len(SPLIT) - 1


def in_hbm(x):
    return pltpu.with_memory_space_constraint(x, pltpu.HBM)


def shaped(shape, dtype=BF):
    return jax.ShapeDtypeStruct(shape, dtype)


def call(kernel, out_shape, in_specs, scratch=(), limit=16, flops=0, nbytes=0, out_specs=None):
    many = isinstance(out_shape, (list, tuple))
    return pl.pallas_call(
        kernel,
        out_shape=out_shape,
        in_specs=in_specs,
        out_specs=out_specs or ([VMEM] * len(out_shape) if many else VMEM),
        scratch_shapes=list(scratch),
        compiler_params=pltpu.CompilerParams(vmem_limit_bytes=limit << 20),
        cost_estimate=pl.CostEstimate(flops=flops, bytes_accessed=nbytes, transcendentals=0),
    )


def short_conv(x, sf_ref, feature, lanes):
    total = sf_ref[feature, 0:1, lanes] * x
    for d in range(1, sf_ref.shape[1]):
        total = total + sf_ref[feature, d : d + 1, lanes] * pltpu.roll(x, d, 0)
    return total


def short_conv_rows(x, rows_ref, sf_ref, feature, lanes):
    tokens = x.shape[0]
    rows_ref[:8, :] = jnp.zeros((8, x.shape[1]), F32)
    rows_ref[8:, :] = x
    total = sf_ref[feature, 0:1, lanes] * x
    for d in range(1, sf_ref.shape[1]):
        total = total + sf_ref[feature, d : d + 1, lanes] * rows_ref[8 - d : 8 - d + tokens, :]
    return total


def pack_kernel(x_hbm, sf_hbm, out_hbm, x_ref, head_ref, tail_ref, sf_ref, out_ref, rows_ref, sems, *, gsize):
    feats, tokens, channels = x_hbm.shape
    parts = channels // 128
    few = 128 // gsize
    firsts = [
        pltpu.make_async_copy(sf_hbm, sf_ref, sems.at[parts]),
        pltpu.make_async_copy(x_hbm.at[0, :EDGE], head_ref, sems.at[parts + 1]),
        pltpu.make_async_copy(x_hbm.at[0, tokens - EDGE :], tail_ref, sems.at[parts + 2]),
    ]
    reads = [
        pltpu.make_async_copy(
            x_hbm.at[1:, :, j * 128 : (j + 1) * 128], x_ref.at[:, :, j * 128 : (j + 1) * 128], sems.at[j]
        )
        for j in range(parts)
    ]
    writes = [
        pltpu.make_async_copy(
            out_ref.at[j * few : (j + 1) * few], out_hbm.at[j * few : (j + 1) * few], sems.at[parts + 3 + j]
        )
        for j in range(parts)
    ]
    for copy in firsts + reads:
        copy.start()
    for copy in firsts:
        copy.wait()
    pad = jnp.zeros((64 - 2 * EDGE * feats, 128), F32)
    left = lax.broadcasted_iota(jnp.int32, (few, 8, 128), 2) < 64
    for j in range(parts):
        lanes = slice(j * 128, (j + 1) * 128)
        groups = slice(j * few, (j + 1) * few)
        reads[j].wait()
        x = [x_ref[f, :, lanes].astype(F32) for f in range(feats - 1)]
        key = short_conv_rows(x[0], rows_ref.at[j, 0], sf_ref, 1, lanes)
        values = key * short_conv_rows(x[1], rows_ref.at[j, 1], sf_ref, 2, lanes)
        out_ref[groups, :gsize, :] = values.T.astype(BF).reshape(few, gsize, tokens)
        edges = [tail_ref[:, lanes].astype(F32), head_ref[:, lanes].astype(F32)]
        for f in range(feats - 1):
            edges += [x[f][tokens - EDGE :], x[f][:EDGE]]
        edges = jnp.concatenate((edges + [pad]) * 2, axis=0).T.reshape(few, gsize, 128)
        out_ref[groups, gsize:, :] = jnp.where(left, edges[:, :8], edges[:, 8:]).astype(BF)
        writes[j].start()
    for copy in writes:
        copy.wait()


def blocks_of(first, own):
    tp = lax.axis_index("tp")
    y = lax.div(tp, 2)
    core = lax.rem(tp, 2)
    if not own:
        core = 1 - core
    near = jnp.bitwise_xor(y, 1)
    far = 3 - y
    even = core == 0
    if first:
        chips = (jnp.where(even, near, far), 3 - near)
    else:
        chips = (y, jnp.where(even, far, near))
    return [chip * 2 + core for chip in chips]


def fetches(w_hbm, w_ref, sems, wanted):
    cols = w_ref.shape[2]
    copies = []
    for slot, block in enumerate(wanted):
        start = pl.multiple_of(block * cols, cols)
        copies.append(pltpu.make_async_copy(w_hbm.at[:, pl.ds(start, cols)], w_ref.at[slot], sems.at[slot]))
    for copy in copies:
        copy.start()
    return copies


def prep_kernel(
    x_hbm, sf_hbm, lf_hbm, w_hbm, g_ref, gate_ref, coef_ref, w_ref, x_ref, sf_ref, lf_ref, sems, w_sems, *, gsize
):
    tok, channels = x_ref.shape
    _, taps, _ = sf_ref.shape
    groups, reach = lf_ref.shape
    lags = reach // tok + 1
    copies = [
        pltpu.make_async_copy(sf_hbm, sf_ref, sems.at[0]),
        pltpu.make_async_copy(lf_hbm, lf_ref, sems.at[1]),
        pltpu.make_async_copy(x_hbm.at[0], x_ref, sems.at[2]),
    ]
    for copy in copies:
        copy.start()
    fetched = fetches(w_hbm, w_ref, w_sems, blocks_of(True, False))
    me = lax.axis_index("ctx")
    for copy in copies:
        copy.wait()
    row = lax.broadcasted_iota(jnp.int32, (8, channels), 0)
    col = lax.broadcasted_iota(jnp.int32, (8, channels), 1)
    lane = lax.broadcasted_iota(jnp.int32, (8, 128), 1)
    for d in range(taps):
        tile = jnp.zeros((8, 128), F32)
        for h in range(2):
            pick = col == row + (me * gsize + 8 * h)
            for f in range(3):
                tap = jnp.sum(jnp.where(pick, sf_ref[f, d : d + 1, :], 0.0), axis=1, keepdims=True)
                tile = jnp.where(lane // 16 == 4 * h + f, jnp.broadcast_to(tap, (8, 128)), tile)
        coef_ref[d] = tile
    s_i = lax.broadcasted_iota(jnp.int32, (tok, tok), 0)
    t_i = lax.broadcasted_iota(jnp.int32, (tok, tok), 1)
    upper = t_i >= s_i
    mine = lax.broadcasted_iota(jnp.int32, (groups, tok), 0) == me
    before = jnp.zeros((tok, tok), F32)
    for k in range(lags):
        if k < lags - 1:
            taps_k = lf_ref[:, k * tok : (k + 1) * tok].astype(F32)
            taps_k = jnp.sum(jnp.where(mine, taps_k, 0.0), axis=0, keepdims=True)
            here = pltpu.roll(jnp.broadcast_to(taps_k, (tok, tok)), 0, 1, stride=1, stride_axis=0)
        else:
            here = jnp.zeros((tok, tok), F32)
        g_ref[k * tok : (k + 1) * tok, :] = jnp.where(upper, here, before).astype(BF)
        before = here
    for j in range(0, channels, 128):
        lanes = slice(j, j + 128)
        gate_ref[:, lanes] = short_conv(x_ref[:, lanes].astype(F32), sf_ref, 0, lanes)
    for copy in fetched:
        copy.wait()


def conv_kernel(x_ref, t_ref, coef_ref, out_ref, z_ref, g_ref, *, gsize):
    blocks, _, tok = x_ref.shape
    taps = coef_ref.shape[0]
    lane = lax.broadcasted_iota(jnp.int32, (blocks, 8, tok), 2)
    edge = x_ref[:, gsize:, :].astype(F32)
    before = jnp.concatenate([jnp.zeros((1, 8, tok), F32), edge[:-1]], axis=0)
    edge = jnp.where(lane % (2 * EDGE) < EDGE, before, edge).reshape(blocks * 8, tok)
    conved = jnp.zeros((blocks, 8, tok), F32)
    for d in range(taps):
        turned = edge if d == 0 else pltpu.roll(edge, d, 1)
        conved = conved + coef_ref[d][None] * turned.reshape(blocks, 8, tok)
    conved = conved.reshape(blocks * 8, tok)

    def at(first):
        return pltpu.roll(conved, tok - first, 1).reshape(blocks, 8, tok)

    gate = jnp.concatenate([at(EDGE), at(64 + EDGE)], axis=1)
    key = jnp.concatenate([at(3 * EDGE), at(64 + 3 * EDGE)], axis=1)
    value = jnp.concatenate([at(5 * EDGE), at(64 + 5 * EDGE)], axis=1)
    head = lax.broadcasted_iota(jnp.int32, (blocks, gsize, tok), 2) < EDGE
    values = jnp.where(head, key * value, x_ref[:, :gsize, :].astype(F32))
    g_ref[:tok, :tok] = jnp.zeros((tok, tok), BF)
    g_ref[tok:, :tok] = t_ref[...]
    g_ref[: t_ref.shape[0], tok:] = t_ref[...]
    g_ref[t_ref.shape[0] :, tok:] = jnp.zeros((tok, tok), BF)
    values = values.astype(BF).reshape(blocks // 2, 2, gsize, tok)
    rows = blocks // 2 * gsize
    for k in range(g_ref.shape[0] // tok):
        source = values[:, 1 - k % 2].reshape(rows, tok)
        skip = k // 2 * gsize
        if skip:
            z_ref[:skip, k * tok : (k + 1) * tok] = jnp.zeros((skip, tok), BF)
        z_ref[skip:, k * tok : (k + 1) * tok] = source[: rows - skip]
    mixed = jnp.dot(z_ref[...], g_ref[...], preferred_element_type=F32).reshape(blocks // 2, gsize, 2 * tok)
    mixed = jnp.stack([mixed[:, :, :tok], mixed[:, :, tok:]], axis=1).reshape(blocks, gsize, tok)
    out_ref[...] = jnp.where(head, gate * mixed, mixed).astype(BF)


def product(ht, weight):
    return jnp.dot(ht, weight, preferred_element_type=F32).astype(BF)


def first_theirs_kernel(h_ref, gate_ref, w_ref, out_ref, ht_ref):
    mixed = h_ref[...].T
    ht_ref[...] = (gate_ref[...] * mixed.astype(F32)).astype(BF)
    ht_ref[:EDGE, :] = mixed[:EDGE]
    for slot in range(2):
        out_ref[slot] = product(ht_ref[...], w_ref[slot])


def fetched_kernel(ht_ref, w_hbm, out_ref, w_ref, sems, *, first, own):
    copies = fetches(w_hbm, w_ref, sems, blocks_of(first, own))
    for slot in range(2):
        copies[slot].wait()
        out_ref[slot] = product(ht_ref[...], w_ref[slot])


def join_kernel(got_ref, own_ref, ht_in_ref, out_ref, ht_ref, *, chunk):
    ht_ref[...] = ht_in_ref[...]
    lanes = slice(SPLIT[chunk], SPLIT[chunk + 1])
    out_ref[...] = (got_ref[:, :, lanes].astype(F32) + own_ref[:, :, lanes].astype(F32)).astype(BF)


def pass_kernel(got_ref, own_ref, in_ref, *refs, chunk):
    out_ref, kept_ref = refs[-2:]
    lanes = slice(SPLIT[chunk], SPLIT[chunk + 1])
    total = got_ref[:, :, lanes].astype(F32) + own_ref[:, :, lanes].astype(F32) + in_ref[...].astype(F32)
    kept_ref[...] = total[0]
    out_ref[...] = total[1].astype(BF)


def finish_kernel(*refs):
    *in_refs, out_ref = refs
    for i in range(CHUNKS):
        total = in_refs[i][...] + in_refs[CHUNKS + i][...].astype(F32)
        out_ref[:, SPLIT[i] : SPLIT[i + 1]] = total.astype(BF)


def body(projected, short_filter, long_filter, out_weight):
    tok, feats, channels = projected.shape
    groups, reach = long_filter.shape
    gsize = channels // groups
    taps = short_filter.shape[0]
    dout = out_weight.shape[1]
    n_tp = lax.axis_size("tp")
    cols = dout // n_tp
    blocks = lax.axis_size("ctx")
    lags = reach // tok + 1

    x = in_hbm(projected.transpose(1, 0, 2))
    sf = in_hbm(short_filter.transpose(1, 0, 2))
    weight = in_hbm(out_weight)
    packed = call(
        functools.partial(pack_kernel, gsize=gsize),
        shaped((groups, gsize + 8, tok)),
        [HBM] * 2,
        scratch=(
            pltpu.VMEM((feats - 1, tok, channels), BF),
            pltpu.VMEM((EDGE, channels), BF),
            pltpu.VMEM((EDGE, channels), BF),
            pltpu.VMEM((feats, taps, channels), F32),
            pltpu.VMEM((groups, gsize + 8, tok), BF),
            pltpu.VMEM((channels // 128, feats - 1, tok + 8, 128), F32),
            pltpu.SemaphoreType.DMA((2 * channels // 128 + 3,)),
        ),
        out_specs=HBM,
    )(x, sf)
    spread = lax.all_to_all(packed, "ctx", 0, 0, tiled=True)
    toeplitz, gate, coef, theirs_weight = call(
        functools.partial(prep_kernel, gsize=gsize),
        [
            shaped((lags * tok, tok)),
            shaped((tok, channels), F32),
            shaped((taps, 8, 128), F32),
            shaped((2, channels, cols)),
        ],
        [HBM] * 4,
        scratch=(
            pltpu.VMEM((tok, channels), BF),
            pltpu.VMEM((feats, taps, channels), F32),
            pltpu.VMEM(long_filter.shape, BF),
            pltpu.SemaphoreType.DMA((3,)),
            pltpu.SemaphoreType.DMA((2,)),
        ),
    )(x, sf, in_hbm(long_filter), weight)
    mixed = call(
        functools.partial(conv_kernel, gsize=gsize),
        shaped((blocks, gsize, tok)),
        [VMEM] * 3,
        scratch=(
            pltpu.VMEM((blocks // 2 * gsize, (lags + 1) * tok), BF),
            pltpu.VMEM(((lags + 1) * tok, 2 * tok), BF),
        ),
    )(spread, toeplitz, coef)
    mixed = lax.all_to_all(mixed, "ctx", 0, 0, tiled=True).reshape(channels, tok)

    def project(ht, first, own):
        return call(
            functools.partial(fetched_kernel, first=first, own=own),
            shaped((2, tok, cols)),
            [VMEM, HBM],
            scratch=(pltpu.VMEM((2, channels, cols), BF), pltpu.SemaphoreType.DMA((2,))),
            flops=4 * tok * channels * cols,
            nbytes=4 * channels * cols,
        )(ht, weight)

    def swap(x, peer):
        return lax.ppermute(x, "tp", [(i, peer(i)) for i in range(n_tp)])

    def partner(i):
        return i ^ 1

    def hop(i, parity):
        return i ^ 2 if (i + parity) % 2 == 0 else (3 - i // 2) * 2 + i % 2

    widths = [SPLIT[i + 1] - SPLIT[i] for i in range(CHUNKS)]
    theirs, ht = call(
        first_theirs_kernel, [shaped((2, tok, cols)), shaped((tok, channels))], [VMEM] * 3
    )(mixed, gate, theirs_weight)
    got = swap(theirs, partner)
    own = project(ht, True, True)
    arrived = []
    for i in range(CHUNKS):
        send, ht = call(
            functools.partial(join_kernel, chunk=i), [shaped((2, tok, widths[i])), shaped((tok, channels))], [VMEM] * 3
        )(got, own, ht)
        arrived.append(swap(send, functools.partial(hop, parity=0)))
    theirs = project(ht, False, False)
    got = swap(theirs, partner)
    own = project(ht, False, True)
    kept, last = [], []
    for i in range(CHUNKS):
        onward, keep = call(
            functools.partial(pass_kernel, chunk=i),
            [shaped((tok, widths[i])), shaped((tok, widths[i]), F32)],
            [VMEM] * (3 + min(i, 1)),
        )(got, own, arrived[i], *kept[-1:])
        kept.append(keep)
        last.append(swap(onward, functools.partial(hop, parity=1)))
    return call(finish_kernel, shaped((tok, cols)), [VMEM] * (2 * CHUNKS))(*kept, *last)


def solution(mesh):
    return jax.shard_map(
        body,
        mesh=mesh,
        in_specs=(P("ctx", None, "tp"), P(None, None, "tp"), P("tp", None), P("tp", None)),
        out_specs=P("ctx", "tp"),
        check_vma=False,
    )
```

```python
import functools

import jax
import jax.numpy as jnp
from jax import lax
from jax.experimental import pallas as pl
from jax.experimental.pallas import tpu as pltpu
from jax.sharding import PartitionSpec as P

BF = jnp.bfloat16
F32 = jnp.float32
VMEM = pl.BlockSpec(memory_space=pltpu.VMEM)
HBM = pl.BlockSpec(memory_space=pltpu.HBM)

EDGE = 8


def in_hbm(x):
    return pltpu.with_memory_space_constraint(x, pltpu.HBM)


def shaped(shape, dtype=BF):
    return jax.ShapeDtypeStruct(shape, dtype)


def call(kernel, out_shape, in_specs, scratch=(), limit=16, flops=0, nbytes=0, out_specs=None):
    many = isinstance(out_shape, (list, tuple))
    return pl.pallas_call(
        kernel,
        out_shape=out_shape,
        in_specs=in_specs,
        out_specs=out_specs or ([VMEM] * len(out_shape) if many else VMEM),
        scratch_shapes=list(scratch),
        compiler_params=pltpu.CompilerParams(vmem_limit_bytes=limit << 20),
        cost_estimate=pl.CostEstimate(flops=flops, bytes_accessed=nbytes, transcendentals=0),
    )


def short_conv(x, sf_ref, feature, lanes):
    total = sf_ref[feature, 0:1, lanes] * x
    for d in range(1, sf_ref.shape[1]):
        total = total + sf_ref[feature, d : d + 1, lanes] * pltpu.roll(x, d, 0)
    return total


def short_conv_rows(x, rows_ref, sf_ref, feature, lanes):
    tokens = x.shape[0]
    rows_ref[:8, :] = jnp.zeros((8, x.shape[1]), F32)
    rows_ref[8:, :] = x
    total = sf_ref[feature, 0:1, lanes] * x
    for d in range(1, sf_ref.shape[1]):
        total = total + sf_ref[feature, d : d + 1, lanes] * rows_ref[8 - d : 8 - d + tokens, :]
    return total


def pack_kernel(x_hbm, sf_hbm, out_hbm, x_ref, head_ref, tail_ref, sf_ref, out_ref, rows_ref, sems, *, gsize):
    feats, tokens, channels = x_hbm.shape
    parts = channels // 128
    few = 128 // gsize
    firsts = [
        pltpu.make_async_copy(sf_hbm, sf_ref, sems.at[parts]),
        pltpu.make_async_copy(x_hbm.at[0, :EDGE], head_ref, sems.at[parts + 1]),
        pltpu.make_async_copy(x_hbm.at[0, tokens - EDGE :], tail_ref, sems.at[parts + 2]),
    ]
    reads = [
        pltpu.make_async_copy(
            x_hbm.at[1:, :, j * 128 : (j + 1) * 128], x_ref.at[:, :, j * 128 : (j + 1) * 128], sems.at[j]
        )
        for j in range(parts)
    ]
    writes = [
        pltpu.make_async_copy(
            out_ref.at[j * few : (j + 1) * few], out_hbm.at[j * few : (j + 1) * few], sems.at[parts + 3 + j]
        )
        for j in range(parts)
    ]
    for copy in firsts + reads:
        copy.start()
    for copy in firsts:
        copy.wait()
    pad = jnp.zeros((64 - 2 * EDGE * feats, 128), F32)
    left = lax.broadcasted_iota(jnp.int32, (few, 8, 128), 2) < 64
    for j in range(parts):
        lanes = slice(j * 128, (j + 1) * 128)
        groups = slice(j * few, (j + 1) * few)
        reads[j].wait()
        x = [x_ref[f, :, lanes].astype(F32) for f in range(feats - 1)]
        key = short_conv_rows(x[0], rows_ref.at[j, 0], sf_ref, 1, lanes)
        values = key * short_conv_rows(x[1], rows_ref.at[j, 1], sf_ref, 2, lanes)
        out_ref[groups, :gsize, :] = values.T.astype(BF).reshape(few, gsize, tokens)
        edges = [tail_ref[:, lanes].astype(F32), head_ref[:, lanes].astype(F32)]
        for f in range(feats - 1):
            edges += [x[f][tokens - EDGE :], x[f][:EDGE]]
        edges = jnp.concatenate((edges + [pad]) * 2, axis=0).T.reshape(few, gsize, 128)
        out_ref[groups, gsize:, :] = jnp.where(left, edges[:, :8], edges[:, 8:]).astype(BF)
        writes[j].start()
    for copy in writes:
        copy.wait()


def blocks_of(first, own):
    tp = lax.axis_index("tp")
    y = lax.div(tp, 2)
    core = lax.rem(tp, 2)
    if not own:
        core = 1 - core
    near = jnp.bitwise_xor(y, 1)
    far = 3 - y
    even = core == 0
    if first:
        chips = (jnp.where(even, near, far), 3 - near)
    else:
        chips = (y, jnp.where(even, far, near))
    return [chip * 2 + core for chip in chips]


def fetches(w_hbm, w_ref, sems, wanted):
    cols = w_ref.shape[2]
    copies = []
    for slot, block in enumerate(wanted):
        start = pl.multiple_of(block * cols, cols)
        copies.append(pltpu.make_async_copy(w_hbm.at[:, pl.ds(start, cols)], w_ref.at[slot], sems.at[slot]))
    for copy in copies:
        copy.start()
    return copies


def prep_kernel(
    x_hbm, sf_hbm, lf_hbm, w_hbm, g_ref, gate_ref, coef_ref, w_ref, x_ref, sf_ref, lf_ref, sems, w_sems, *, gsize
):
    tok, channels = x_ref.shape
    _, taps, _ = sf_ref.shape
    groups, reach = lf_ref.shape
    lags = reach // tok + 1
    copies = [
        pltpu.make_async_copy(sf_hbm, sf_ref, sems.at[0]),
        pltpu.make_async_copy(lf_hbm, lf_ref, sems.at[1]),
        pltpu.make_async_copy(x_hbm.at[0], x_ref, sems.at[2]),
    ]
    for copy in copies:
        copy.start()
    fetched = fetches(w_hbm, w_ref, w_sems, blocks_of(True, False))
    me = lax.axis_index("ctx")
    for copy in copies:
        copy.wait()
    row = lax.broadcasted_iota(jnp.int32, (8, channels), 0)
    col = lax.broadcasted_iota(jnp.int32, (8, channels), 1)
    lane = lax.broadcasted_iota(jnp.int32, (8, 128), 1)
    for d in range(taps):
        tile = jnp.zeros((8, 128), F32)
        for h in range(2):
            pick = col == row + (me * gsize + 8 * h)
            for f in range(3):
                tap = jnp.sum(jnp.where(pick, sf_ref[f, d : d + 1, :], 0.0), axis=1, keepdims=True)
                tile = jnp.where(lane // 16 == 4 * h + f, jnp.broadcast_to(tap, (8, 128)), tile)
        coef_ref[d] = tile
    s_i = lax.broadcasted_iota(jnp.int32, (tok, tok), 0)
    t_i = lax.broadcasted_iota(jnp.int32, (tok, tok), 1)
    upper = t_i >= s_i
    mine = lax.broadcasted_iota(jnp.int32, (groups, tok), 0) == me
    before = jnp.zeros((tok, tok), F32)
    for k in range(lags):
        if k < lags - 1:
            taps_k = lf_ref[:, k * tok : (k + 1) * tok].astype(F32)
            taps_k = jnp.sum(jnp.where(mine, taps_k, 0.0), axis=0, keepdims=True)
            here = pltpu.roll(jnp.broadcast_to(taps_k, (tok, tok)), 0, 1, stride=1, stride_axis=0)
        else:
            here = jnp.zeros((tok, tok), F32)
        g_ref[k * tok : (k + 1) * tok, :] = jnp.where(upper, here, before).astype(BF)
        before = here
    for j in range(0, channels, 128):
        lanes = slice(j, j + 128)
        gate_ref[:, lanes] = short_conv(x_ref[:, lanes].astype(F32), sf_ref, 0, lanes)
    for copy in fetched:
        copy.wait()


def conv_kernel(x_ref, t_ref, coef_ref, out_ref, z_ref, g_ref, *, gsize):
    blocks, _, tok = x_ref.shape
    taps = coef_ref.shape[0]
    lane = lax.broadcasted_iota(jnp.int32, (blocks, 8, tok), 2)
    edge = x_ref[:, gsize:, :].astype(F32)
    before = jnp.concatenate([jnp.zeros((1, 8, tok), F32), edge[:-1]], axis=0)
    edge = jnp.where(lane % (2 * EDGE) < EDGE, before, edge).reshape(blocks * 8, tok)
    conved = jnp.zeros((blocks, 8, tok), F32)
    for d in range(taps):
        turned = edge if d == 0 else pltpu.roll(edge, d, 1)
        conved = conved + coef_ref[d][None] * turned.reshape(blocks, 8, tok)
    conved = conved.reshape(blocks * 8, tok)

    def at(first):
        return pltpu.roll(conved, tok - first, 1).reshape(blocks, 8, tok)

    gate = jnp.concatenate([at(EDGE), at(64 + EDGE)], axis=1)
    key = jnp.concatenate([at(3 * EDGE), at(64 + 3 * EDGE)], axis=1)
    value = jnp.concatenate([at(5 * EDGE), at(64 + 5 * EDGE)], axis=1)
    head = lax.broadcasted_iota(jnp.int32, (blocks, gsize, tok), 2) < EDGE
    values = jnp.where(head, key * value, x_ref[:, :gsize, :].astype(F32))
    g_ref[:tok, :tok] = jnp.zeros((tok, tok), BF)
    g_ref[tok:, :tok] = t_ref[...]
    g_ref[: t_ref.shape[0], tok:] = t_ref[...]
    g_ref[t_ref.shape[0] :, tok:] = jnp.zeros((tok, tok), BF)
    values = values.astype(BF).reshape(blocks // 2, 2, gsize, tok)
    rows = blocks // 2 * gsize
    for k in range(g_ref.shape[0] // tok):
        source = values[:, 1 - k % 2].reshape(rows, tok)
        skip = k // 2 * gsize
        if skip:
            z_ref[:skip, k * tok : (k + 1) * tok] = jnp.zeros((skip, tok), BF)
        z_ref[skip:, k * tok : (k + 1) * tok] = source[: rows - skip]
    mixed = jnp.dot(z_ref[...], g_ref[...], preferred_element_type=F32).reshape(blocks // 2, gsize, 2 * tok)
    mixed = jnp.stack([mixed[:, :, :tok], mixed[:, :, tok:]], axis=1).reshape(blocks, gsize, tok)
    out_ref[...] = jnp.where(head, gate * mixed, mixed).astype(BF)


def product(ht, weight):
    return jnp.dot(ht, weight, preferred_element_type=F32).astype(BF)


def first_theirs_kernel(h_ref, gate_ref, w_ref, out_ref, ht_ref):
    mixed = h_ref[...].T
    ht_ref[...] = (gate_ref[...] * mixed.astype(F32)).astype(BF)
    ht_ref[:EDGE, :] = mixed[:EDGE]
    out_ref[...] = product(ht_ref[...], w_ref[1])


def first_own_kernel(ht_ref, theirs_ref, w_hbm, own_ref, out_ref, w_ref, sems):
    copies = fetches(w_hbm, w_ref, sems, blocks_of(True, True)[1:])
    out_ref[...] = product(ht_ref[...], theirs_ref[0])
    copies[0].wait()
    own_ref[...] = product(ht_ref[...], w_ref[0])


def fetched_kernel(ht_ref, w_hbm, *refs, wanted):
    *out_refs, w_ref, sems = refs
    copies = fetches(w_hbm, w_ref, sems, [blocks_of(first, own)[slot] for first, own, slot in wanted])
    for copy, out_ref, slot in zip(copies, out_refs, range(len(wanted))):
        copy.wait()
        out_ref[...] = product(ht_ref[...], w_ref[slot])


def join_kernel(got_ref, own_ref, ht_in_ref, out_ref, ht_ref):
    ht_ref[...] = ht_in_ref[...]
    out_ref[...] = (got_ref[...].astype(F32) + own_ref[...].astype(F32)).astype(BF)


def pass_kernel(got_ref, own_ref, in_ref, ht_in_ref, out_ref, ht_ref):
    ht_ref[...] = ht_in_ref[...]
    total = got_ref[...].astype(F32) + own_ref[...].astype(F32) + in_ref[...].astype(F32)
    out_ref[...] = total.astype(BF)


def keep_kernel(got_ref, own_ref, in_ref, kept_ref):
    kept_ref[...] = got_ref[...].astype(F32) + own_ref[...].astype(F32) + in_ref[...].astype(F32)


def finish_kernel(kept_ref, in_ref, out_ref):
    out_ref[...] = (kept_ref[...] + in_ref[...].astype(F32)).astype(BF)


def body(projected, short_filter, long_filter, out_weight):
    tok, feats, channels = projected.shape
    groups, reach = long_filter.shape
    gsize = channels // groups
    taps = short_filter.shape[0]
    dout = out_weight.shape[1]
    n_tp = lax.axis_size("tp")
    cols = dout // n_tp
    blocks = lax.axis_size("ctx")
    lags = reach // tok + 1

    x = in_hbm(projected.transpose(1, 0, 2))
    sf = in_hbm(short_filter.transpose(1, 0, 2))
    weight = in_hbm(out_weight)
    packed = call(
        functools.partial(pack_kernel, gsize=gsize),
        shaped((groups, gsize + 8, tok)),
        [HBM] * 2,
        scratch=(
            pltpu.VMEM((feats - 1, tok, channels), BF),
            pltpu.VMEM((EDGE, channels), BF),
            pltpu.VMEM((EDGE, channels), BF),
            pltpu.VMEM((feats, taps, channels), F32),
            pltpu.VMEM((groups, gsize + 8, tok), BF),
            pltpu.VMEM((channels // 128, feats - 1, tok + 8, 128), F32),
            pltpu.SemaphoreType.DMA((2 * channels // 128 + 3,)),
        ),
        out_specs=HBM,
    )(x, sf)
    spread = lax.all_to_all(packed, "ctx", 0, 0, tiled=True)
    toeplitz, gate, coef, theirs_weight = call(
        functools.partial(prep_kernel, gsize=gsize),
        [
            shaped((lags * tok, tok)),
            shaped((tok, channels), F32),
            shaped((taps, 8, 128), F32),
            shaped((2, channels, cols)),
        ],
        [HBM] * 4,
        scratch=(
            pltpu.VMEM((tok, channels), BF),
            pltpu.VMEM((feats, taps, channels), F32),
            pltpu.VMEM(long_filter.shape, BF),
            pltpu.SemaphoreType.DMA((3,)),
            pltpu.SemaphoreType.DMA((2,)),
        ),
    )(x, sf, in_hbm(long_filter), weight)
    mixed = call(
        functools.partial(conv_kernel, gsize=gsize),
        shaped((blocks, gsize, tok)),
        [VMEM] * 3,
        scratch=(
            pltpu.VMEM((blocks // 2 * gsize, (lags + 1) * tok), BF),
            pltpu.VMEM(((lags + 1) * tok, 2 * tok), BF),
        ),
    )(spread, toeplitz, coef)
    mixed = lax.all_to_all(mixed, "ctx", 0, 0, tiled=True).reshape(channels, tok)

    def project(ht, wanted):
        count = len(wanted)
        return call(
            functools.partial(fetched_kernel, wanted=wanted),
            [shaped((tok, cols))] * count,
            [VMEM, HBM],
            scratch=(pltpu.VMEM((count, channels, cols), BF), pltpu.SemaphoreType.DMA((count,))),
            flops=2 * count * tok * channels * cols,
            nbytes=2 * count * channels * cols,
        )(ht, weight)

    def swap(x, peer):
        return lax.ppermute(x, "tp", [(i, peer(i)) for i in range(n_tp)])

    def partner(i):
        return i ^ 1

    def hop(i, parity):
        return i ^ 2 if (i + parity) % 2 == 0 else (3 - i // 2) * 2 + i % 2

    block = shaped((tok, cols))
    rows = shaped((tok, channels))
    near_hop = functools.partial(hop, parity=0)
    far_hop = functools.partial(hop, parity=1)

    theirs, ht = call(first_theirs_kernel, [block, rows], [VMEM] * 3)(mixed, gate, theirs_weight)
    got = swap(theirs, partner)
    own, theirs = call(
        first_own_kernel,
        [block] * 2,
        [VMEM] * 2 + [HBM],
        scratch=(pltpu.VMEM((1, channels, cols), BF), pltpu.SemaphoreType.DMA((1,))),
    )(ht, theirs_weight, weight)
    send, ht = call(join_kernel, [block, rows], [VMEM] * 3)(got, own, ht)
    onward = swap(send, near_hop)

    got = swap(theirs, partner)
    own, theirs = project(ht, ((True, True, 0), (False, False, 1)))
    send, ht = call(join_kernel, [block, rows], [VMEM] * 3)(got, own, ht)
    stayed = swap(send, near_hop)
    got = swap(theirs, partner)
    (own,) = project(ht, ((False, True, 1),))
    send, ht = call(pass_kernel, [block, rows], [VMEM] * 4)(got, own, onward, ht)
    last = swap(send, far_hop)

    theirs, own = project(ht, ((False, False, 0), (False, True, 0)))
    got = swap(theirs, partner)
    kept = call(keep_kernel, shaped((tok, cols), F32), [VMEM] * 3)(got, own, stayed)
    return call(finish_kernel, block, [VMEM] * 2)(kept, last)


def solution(mesh):
    return jax.shard_map(
        body,
        mesh=mesh,
        in_specs=(P("ctx", None, "tp"), P(None, None, "tp"), P("tp", None), P("tp", None)),
        out_specs=P("ctx", "tp"),
        check_vma=False,
    )
```

```python
import functools

import jax
import jax.numpy as jnp
from jax import lax
from jax.experimental import pallas as pl
from jax.experimental.pallas import tpu as pltpu
from jax.sharding import PartitionSpec as P

BF = jnp.bfloat16
F32 = jnp.float32
VMEM = pl.BlockSpec(memory_space=pltpu.VMEM)
HBM = pl.BlockSpec(memory_space=pltpu.HBM)

EDGE = 8
EARLY = 384


def in_hbm(x):
    return pltpu.with_memory_space_constraint(x, pltpu.HBM)


def shaped(shape, dtype=BF):
    return jax.ShapeDtypeStruct(shape, dtype)


def call(kernel, out_shape, in_specs, scratch=(), limit=16, flops=0, nbytes=0, out_specs=None):
    many = isinstance(out_shape, (list, tuple))
    return pl.pallas_call(
        kernel,
        out_shape=out_shape,
        in_specs=in_specs,
        out_specs=out_specs or ([VMEM] * len(out_shape) if many else VMEM),
        scratch_shapes=list(scratch),
        compiler_params=pltpu.CompilerParams(vmem_limit_bytes=limit << 20),
        cost_estimate=pl.CostEstimate(flops=flops, bytes_accessed=nbytes, transcendentals=0),
    )


def short_conv(x, sf_ref, feature, lanes):
    total = sf_ref[feature, 0:1, lanes] * x
    for d in range(1, sf_ref.shape[1]):
        total = total + sf_ref[feature, d : d + 1, lanes] * pltpu.roll(x, d, 0)
    return total


def short_conv_rows(x, rows_ref, sf_ref, feature, lanes):
    tokens = x.shape[0]
    rows_ref[:8, :] = jnp.zeros((8, x.shape[1]), F32)
    rows_ref[8:, :] = x
    total = sf_ref[feature, 0:1, lanes] * x
    for d in range(1, sf_ref.shape[1]):
        total = total + sf_ref[feature, d : d + 1, lanes] * rows_ref[8 - d : 8 - d + tokens, :]
    return total


def pack_kernel(x_hbm, sf_hbm, out_hbm, x_ref, head_ref, tail_ref, sf_ref, out_ref, rows_ref, sems, *, gsize):
    feats, tokens, channels = x_hbm.shape
    parts = channels // 128
    few = 128 // gsize
    firsts = [
        pltpu.make_async_copy(sf_hbm, sf_ref, sems.at[parts]),
        pltpu.make_async_copy(x_hbm.at[0, :EDGE], head_ref, sems.at[parts + 1]),
        pltpu.make_async_copy(x_hbm.at[0, tokens - EDGE :], tail_ref, sems.at[parts + 2]),
    ]
    reads = [
        pltpu.make_async_copy(
            x_hbm.at[1:, :, j * 128 : (j + 1) * 128], x_ref.at[:, :, j * 128 : (j + 1) * 128], sems.at[j]
        )
        for j in range(parts)
    ]
    writes = [
        pltpu.make_async_copy(
            out_ref.at[j * few : (j + 1) * few], out_hbm.at[j * few : (j + 1) * few], sems.at[parts + 3 + j]
        )
        for j in range(parts)
    ]
    for copy in firsts + reads:
        copy.start()
    for copy in firsts:
        copy.wait()
    pad = jnp.zeros((64 - 2 * EDGE * feats, 128), F32)
    left = lax.broadcasted_iota(jnp.int32, (few, 8, 128), 2) < 64
    for j in range(parts):
        lanes = slice(j * 128, (j + 1) * 128)
        groups = slice(j * few, (j + 1) * few)
        reads[j].wait()
        x = [x_ref[f, :, lanes].astype(F32) for f in range(feats - 1)]
        key = short_conv_rows(x[0], rows_ref.at[j, 0], sf_ref, 1, lanes)
        values = key * short_conv_rows(x[1], rows_ref.at[j, 1], sf_ref, 2, lanes)
        out_ref[groups, :gsize, :] = values.T.astype(BF).reshape(few, gsize, tokens)
        edges = [tail_ref[:, lanes].astype(F32), head_ref[:, lanes].astype(F32)]
        for f in range(feats - 1):
            edges += [x[f][tokens - EDGE :], x[f][:EDGE]]
        edges = jnp.concatenate((edges + [pad]) * 2, axis=0).T.reshape(few, gsize, 128)
        out_ref[groups, gsize:, :] = jnp.where(left, edges[:, :8], edges[:, 8:]).astype(BF)
        writes[j].start()
    for copy in writes:
        copy.wait()


def blocks_of(first, own):
    tp = lax.axis_index("tp")
    y = lax.div(tp, 2)
    core = lax.rem(tp, 2)
    if not own:
        core = 1 - core
    near = jnp.bitwise_xor(y, 1)
    far = 3 - y
    even = core == 0
    if first:
        chips = (jnp.where(even, near, far), 3 - near)
    else:
        chips = (y, jnp.where(even, far, near))
    return [chip * 2 + core for chip in chips]


def fetches(w_hbm, w_ref, sems, wanted):
    cols = w_ref.shape[2]
    copies = []
    for slot, block in enumerate(wanted):
        start = pl.multiple_of(block * cols, cols)
        copies.append(pltpu.make_async_copy(w_hbm.at[:, pl.ds(start, cols)], w_ref.at[slot], sems.at[slot]))
    for copy in copies:
        copy.start()
    return copies


def prep_kernel(
    x_hbm, sf_hbm, lf_hbm, w_hbm, g_ref, gate_ref, coef_ref, w_ref, early_ref, x_ref, sf_ref, lf_ref, sems, w_sems, *, gsize
):
    tok, channels = x_ref.shape
    _, taps, _ = sf_ref.shape
    groups, reach = lf_ref.shape
    lags = reach // tok + 1
    copies = [
        pltpu.make_async_copy(sf_hbm, sf_ref, sems.at[0]),
        pltpu.make_async_copy(lf_hbm, lf_ref, sems.at[1]),
        pltpu.make_async_copy(x_hbm.at[0], x_ref, sems.at[2]),
    ]
    for copy in copies:
        copy.start()
    fetched = fetches(w_hbm, w_ref, w_sems, blocks_of(True, False))
    start = pl.multiple_of(blocks_of(True, True)[1] * w_ref.shape[2], 128)
    fetched.append(pltpu.make_async_copy(w_hbm.at[:, pl.ds(start, EARLY)], early_ref, w_sems.at[2]))
    fetched[2].start()
    me = lax.axis_index("ctx")
    for copy in copies:
        copy.wait()
    row = lax.broadcasted_iota(jnp.int32, (8, channels), 0)
    col = lax.broadcasted_iota(jnp.int32, (8, channels), 1)
    lane = lax.broadcasted_iota(jnp.int32, (8, 128), 1)
    for d in range(taps):
        tile = jnp.zeros((8, 128), F32)
        for h in range(2):
            pick = col == row + (me * gsize + 8 * h)
            for f in range(3):
                tap = jnp.sum(jnp.where(pick, sf_ref[f, d : d + 1, :], 0.0), axis=1, keepdims=True)
                tile = jnp.where(lane // 16 == 4 * h + f, jnp.broadcast_to(tap, (8, 128)), tile)
        coef_ref[d] = tile
    s_i = lax.broadcasted_iota(jnp.int32, (tok, tok), 0)
    t_i = lax.broadcasted_iota(jnp.int32, (tok, tok), 1)
    upper = t_i >= s_i
    mine = lax.broadcasted_iota(jnp.int32, (groups, tok), 0) == me
    before = jnp.zeros((tok, tok), F32)
    for k in range(lags):
        if k < lags - 1:
            taps_k = lf_ref[:, k * tok : (k + 1) * tok].astype(F32)
            taps_k = jnp.sum(jnp.where(mine, taps_k, 0.0), axis=0, keepdims=True)
            here = pltpu.roll(jnp.broadcast_to(taps_k, (tok, tok)), 0, 1, stride=1, stride_axis=0)
        else:
            here = jnp.zeros((tok, tok), F32)
        g_ref[k * tok : (k + 1) * tok, :] = jnp.where(upper, here, before).astype(BF)
        before = here
    for j in range(0, channels, 128):
        lanes = slice(j, j + 128)
        gate_ref[:, lanes] = short_conv(x_ref[:, lanes].astype(F32), sf_ref, 0, lanes)
    for copy in fetched:
        copy.wait()


def conv_kernel(x_ref, t_ref, coef_ref, out_ref, z_ref, g_ref, *, gsize):
    blocks, _, tok = x_ref.shape
    taps = coef_ref.shape[0]
    lane = lax.broadcasted_iota(jnp.int32, (blocks, 8, tok), 2)
    edge = x_ref[:, gsize:, :].astype(F32)
    before = jnp.concatenate([jnp.zeros((1, 8, tok), F32), edge[:-1]], axis=0)
    edge = jnp.where(lane % (2 * EDGE) < EDGE, before, edge).reshape(blocks * 8, tok)
    conved = jnp.zeros((blocks, 8, tok), F32)
    for d in range(taps):
        turned = edge if d == 0 else pltpu.roll(edge, d, 1)
        conved = conved + coef_ref[d][None] * turned.reshape(blocks, 8, tok)
    conved = conved.reshape(blocks * 8, tok)

    def at(first):
        return pltpu.roll(conved, tok - first, 1).reshape(blocks, 8, tok)

    gate = jnp.concatenate([at(EDGE), at(64 + EDGE)], axis=1)
    key = jnp.concatenate([at(3 * EDGE), at(64 + 3 * EDGE)], axis=1)
    value = jnp.concatenate([at(5 * EDGE), at(64 + 5 * EDGE)], axis=1)
    head = lax.broadcasted_iota(jnp.int32, (blocks, gsize, tok), 2) < EDGE
    values = jnp.where(head, key * value, x_ref[:, :gsize, :].astype(F32))
    g_ref[:tok, :tok] = jnp.zeros((tok, tok), BF)
    g_ref[tok:, :tok] = t_ref[...]
    g_ref[: t_ref.shape[0], tok:] = t_ref[...]
    g_ref[t_ref.shape[0] :, tok:] = jnp.zeros((tok, tok), BF)
    values = values.astype(BF).reshape(blocks // 2, 2, gsize, tok)
    rows = blocks // 2 * gsize
    for k in range(g_ref.shape[0] // tok):
        source = values[:, 1 - k % 2].reshape(rows, tok)
        skip = k // 2 * gsize
        if skip:
            z_ref[:skip, k * tok : (k + 1) * tok] = jnp.zeros((skip, tok), BF)
        z_ref[skip:, k * tok : (k + 1) * tok] = source[: rows - skip]
    mixed = jnp.dot(z_ref[...], g_ref[...], preferred_element_type=F32).reshape(blocks // 2, gsize, 2 * tok)
    mixed = jnp.stack([mixed[:, :, :tok], mixed[:, :, tok:]], axis=1).reshape(blocks, gsize, tok)
    out_ref[...] = jnp.where(head, gate * mixed, mixed).astype(BF)


def product(ht, weight):
    return jnp.dot(ht, weight, preferred_element_type=F32).astype(BF)


def first_theirs_kernel(h_ref, gate_ref, w_ref, out_ref, ht_ref):
    mixed = h_ref[...].T
    ht_ref[...] = (gate_ref[...] * mixed.astype(F32)).astype(BF)
    ht_ref[:EDGE, :] = mixed[:EDGE]
    out_ref[...] = product(ht_ref[...], w_ref[1])


def first_own_kernel(ht_ref, theirs_ref, early_ref, w_hbm, own_ref, out_ref, w_ref, sem):
    rest = w_ref.shape[1]
    start = pl.multiple_of(blocks_of(True, True)[1] * (EARLY + rest) + EARLY, 128)
    copy = pltpu.make_async_copy(w_hbm.at[:, pl.ds(start, rest)], w_ref, sem)
    copy.start()
    out_ref[...] = product(ht_ref[...], theirs_ref[0])
    own_ref[:, :EARLY] = product(ht_ref[...], early_ref[...])
    copy.wait()
    own_ref[:, EARLY:] = product(ht_ref[...], w_ref[...])


def fetched_kernel(ht_ref, w_hbm, *refs, wanted):
    *out_refs, w_ref, sems = refs
    copies = fetches(w_hbm, w_ref, sems, [blocks_of(first, own)[slot] for first, own, slot in wanted])
    for copy, out_ref, slot in zip(copies, out_refs, range(len(wanted))):
        copy.wait()
        out_ref[...] = product(ht_ref[...], w_ref[slot])


def join_kernel(got_ref, own_ref, ht_in_ref, out_ref, ht_ref):
    ht_ref[...] = ht_in_ref[...]
    out_ref[...] = (got_ref[...].astype(F32) + own_ref[...].astype(F32)).astype(BF)


def pass_kernel(got_ref, own_ref, in_ref, ht_in_ref, out_ref, ht_ref):
    ht_ref[...] = ht_in_ref[...]
    total = got_ref[...].astype(F32) + own_ref[...].astype(F32) + in_ref[...].astype(F32)
    out_ref[...] = total.astype(BF)


def keep_kernel(got_ref, own_ref, in_ref, kept_ref):
    kept_ref[...] = got_ref[...].astype(F32) + own_ref[...].astype(F32) + in_ref[...].astype(F32)


def finish_kernel(kept_ref, in_ref, out_ref):
    out_ref[...] = (kept_ref[...] + in_ref[...].astype(F32)).astype(BF)


def body(projected, short_filter, long_filter, out_weight):
    tok, feats, channels = projected.shape
    groups, reach = long_filter.shape
    gsize = channels // groups
    taps = short_filter.shape[0]
    dout = out_weight.shape[1]
    n_tp = lax.axis_size("tp")
    cols = dout // n_tp
    blocks = lax.axis_size("ctx")
    lags = reach // tok + 1

    x = in_hbm(projected.transpose(1, 0, 2))
    sf = in_hbm(short_filter.transpose(1, 0, 2))
    weight = in_hbm(out_weight)
    packed = call(
        functools.partial(pack_kernel, gsize=gsize),
        shaped((groups, gsize + 8, tok)),
        [HBM] * 2,
        scratch=(
            pltpu.VMEM((feats - 1, tok, channels), BF),
            pltpu.VMEM((EDGE, channels), BF),
            pltpu.VMEM((EDGE, channels), BF),
            pltpu.VMEM((feats, taps, channels), F32),
            pltpu.VMEM((groups, gsize + 8, tok), BF),
            pltpu.VMEM((channels // 128, feats - 1, tok + 8, 128), F32),
            pltpu.SemaphoreType.DMA((2 * channels // 128 + 3,)),
        ),
        out_specs=HBM,
    )(x, sf)
    spread = lax.all_to_all(packed, "ctx", 0, 0, tiled=True)
    toeplitz, gate, coef, theirs_weight, early = call(
        functools.partial(prep_kernel, gsize=gsize),
        [
            shaped((lags * tok, tok)),
            shaped((tok, channels), F32),
            shaped((taps, 8, 128), F32),
            shaped((2, channels, cols)),
            shaped((channels, EARLY)),
        ],
        [HBM] * 4,
        scratch=(
            pltpu.VMEM((tok, channels), BF),
            pltpu.VMEM((feats, taps, channels), F32),
            pltpu.VMEM(long_filter.shape, BF),
            pltpu.SemaphoreType.DMA((3,)),
            pltpu.SemaphoreType.DMA((3,)),
        ),
    )(x, sf, in_hbm(long_filter), weight)
    mixed = call(
        functools.partial(conv_kernel, gsize=gsize),
        shaped((blocks, gsize, tok)),
        [VMEM] * 3,
        scratch=(
            pltpu.VMEM((blocks // 2 * gsize, (lags + 1) * tok), BF),
            pltpu.VMEM(((lags + 1) * tok, 2 * tok), BF),
        ),
    )(spread, toeplitz, coef)
    mixed = lax.all_to_all(mixed, "ctx", 0, 0, tiled=True).reshape(channels, tok)

    def project(ht, wanted):
        count = len(wanted)
        return call(
            functools.partial(fetched_kernel, wanted=wanted),
            [shaped((tok, cols))] * count,
            [VMEM, HBM],
            scratch=(pltpu.VMEM((count, channels, cols), BF), pltpu.SemaphoreType.DMA((count,))),
            flops=2 * count * tok * channels * cols,
            nbytes=2 * count * channels * cols,
        )(ht, weight)

    def swap(x, peer):
        return lax.ppermute(x, "tp", [(i, peer(i)) for i in range(n_tp)])

    def partner(i):
        return i ^ 1

    def hop(i, parity):
        return i ^ 2 if (i + parity) % 2 == 0 else (3 - i // 2) * 2 + i % 2

    block = shaped((tok, cols))
    rows = shaped((tok, channels))
    near_hop = functools.partial(hop, parity=0)
    far_hop = functools.partial(hop, parity=1)

    theirs, ht = call(first_theirs_kernel, [block, rows], [VMEM] * 3)(mixed, gate, theirs_weight)
    got = swap(theirs, partner)
    own, theirs = call(
        first_own_kernel,
        [block] * 2,
        [VMEM] * 3 + [HBM],
        scratch=(pltpu.VMEM((channels, cols - EARLY), BF), pltpu.SemaphoreType.DMA),
    )(ht, theirs_weight, early, weight)
    send, ht = call(join_kernel, [block, rows], [VMEM] * 3)(got, own, ht)
    onward = swap(send, near_hop)

    got = swap(theirs, partner)
    own, theirs = project(ht, ((True, True, 0), (False, False, 1)))
    send, ht = call(join_kernel, [block, rows], [VMEM] * 3)(got, own, ht)
    stayed = swap(send, near_hop)
    got = swap(theirs, partner)
    (own,) = project(ht, ((False, True, 1),))
    send, ht = call(pass_kernel, [block, rows], [VMEM] * 4)(got, own, onward, ht)
    last = swap(send, far_hop)

    theirs, own = project(ht, ((False, False, 0), (False, True, 0)))
    got = swap(theirs, partner)
    kept = call(keep_kernel, shaped((tok, cols), F32), [VMEM] * 3)(got, own, stayed)
    return call(finish_kernel, block, [VMEM] * 2)(kept, last)


def solution(mesh):
    return jax.shard_map(
        body,
        mesh=mesh,
        in_specs=(P("ctx", None, "tp"), P(None, None, "tp"), P("tp", None), P("tp", None)),
        out_specs=P("ctx", "tp"),
        check_vma=False,
    )
```
